128 devices in a mesh: space: 32 (over y, x, core), snap: 4 (over z).
Axes of the slice: x: 4, y: 4, z: 4, core: 2. Of those that a mesh axis runs over, the one named last changes fastest.
Arguments:
- owned_x: bfloat16 [4096, 128, 512], P('space', None, 'snap'), may hold values from -600 to 600
- owned_y: bfloat16 [4096, 128, 512], P('space', None, 'snap'), may hold values from -6 to 6
- patch_dest: int32 [4096], P('space'), may hold values from -1 to 2047, as said below
Outputs:
- q_basis: float32 [2048, 128, 512], P('space', 'snap')
- r_factor: float32 [512, 512], replicated
- projection: float32 [512, 512], replicated
The draws below stay inside these ranges and needn't reach their ends.
Inputs may be any that keep to these rules, and one draw needn't show every extreme that they name: `patch_dest`: every row block 0 to 2047 is named by exactly one slot; -1 marks an empty slot. The 128 slots of one owner (one aligned block of 128 slots) name at most 4 row blocks of any one slab d * 64 to (d + 1) * 64 - 1, and some owner names exactly 4 of every slab.
All inputs are finite; a program needn't handle non-finite values.
Results may differ from the reference program's by a relative error of at most 0.0003.
Values may be sent and summed in bfloat16 or wider, within the bound.
A program may use at most 128 MiB of HBM per device.

```python
import math
import jax
import jax.numpy as jnp
from jax import lax

K = 512
PATCH = 128
BLK_DEV = 64
OWNED = 4096
ROW_BLOCKS = 2048
ROWS = 262144
N_SPACE = 32


def draw_patch_dest(key, part):
    subkeys = jax.random.split(key, 5)
    moved_load = jax.random.randint(subkeys[0], (N_SPACE // 2,), 0, BLK_DEV + 1).at[0].set(BLK_DEV)
    owner_loads = jnp.stack([BLK_DEV + moved_load, BLK_DEV - moved_load], axis=1).reshape(N_SPACE)
    load_ends = jnp.cumsum(owner_loads)
    starts = load_ends - owner_loads
    position = jnp.arange(N_SPACE * BLK_DEV, dtype=jnp.int32)
    virtual = jnp.sum((load_ends[None, :] <= position[:, None]).astype(jnp.int32), axis=1)
    within = position - starts[virtual]
    owner_of = jax.random.permutation(subkeys[1], N_SPACE)
    slab_of = jax.random.permutation(subkeys[2], N_SPACE)
    inner_perm = jax.vmap(lambda sub: jax.random.permutation(sub, BLK_DEV))(jax.random.split(subkeys[3], N_SPACE))
    slot_perm = jax.vmap(lambda sub: jax.random.permutation(sub, 2 * BLK_DEV))(jax.random.split(subkeys[4], N_SPACE))
    source = owner_of[virtual]
    slot_index = slot_perm[source, within]
    slab_index = slab_of[position % N_SPACE]
    block_index = slab_index * BLK_DEV + inner_perm[slab_index, position // N_SPACE]
    empty_list = jnp.full((N_SPACE * 2 * BLK_DEV,), -1, jnp.int32)
    return empty_list.at[source * (2 * BLK_DEV) + slot_index].set(block_index.astype(jnp.int32))


def draw_owned_x(key, part):
    subkeys = jax.random.split(key, 5)
    taps = 12
    noise = jax.random.truncated_normal(subkeys[0], -4.0, 4.0, (OWNED, PATCH, K + taps), jnp.float32)
    memory = jax.random.uniform(subkeys[4], (K,), jnp.float32, 0.3, 0.9)
    values = noise[:, :, taps:]
    for lag in range(1, taps + 1):
        values = values + memory ** lag * noise[:, :, taps - lag:taps - lag + K]
    col_scale = jnp.exp(jax.random.uniform(subkeys[1], (K,), jnp.float32, 0.0, math.log(4.0)))
    mixed = values * col_scale
    return jnp.clip(mixed, -600.0, 600.0).astype(jnp.bfloat16)


def level_of(own_key, extent, cuts, least, largest):
    gain, own = 1.0, jax.random.fold_in(own_key, 6)
    for dim, shards_of in cuts:
        heights = jnp.exp(jax.random.uniform(jax.random.fold_in(own, dim), (shards_of,), jnp.float32, least / len(cuts), largest / len(cuts)))
        gain = gain * jnp.repeat(heights, extent[dim] // shards_of).reshape([-1 if axis == dim else 1 for axis in range(len(extent))])
    return gain


def gaussian(rng, shape, spread, bound, shards=(), kind=jnp.bfloat16):
    loudness = level_of(rng, shape, shards, -0.22, 0.18) if shards else 1.0
    drawn = jax.random.normal(rng, shape, jnp.float32) * spread * loudness
    return jnp.minimum(jnp.maximum(drawn, -bound), bound).astype(kind)


def setup_inputs(seed: int = 0) -> dict:
    key_list = jax.random.split(jax.random.key(seed), 4)
    return {
        "owned_x": draw_owned_x(jax.random.fold_in(key_list[3], 71), 0),
        "owned_y": gaussian(key_list[1], (OWNED, PATCH, K), 1.0, 6.0, ((0, 32), (2, 4))),
        "patch_dest": draw_patch_dest(jax.random.fold_in(key_list[3], 71), 0),
    }


def place_blocks(owned, patch_dest):
    target = jnp.where(patch_dest >= 0, patch_dest, ROW_BLOCKS).astype(jnp.int32)
    empty_slab = jnp.zeros((ROW_BLOCKS, PATCH, K), owned.dtype)
    return empty_slab.at[target].set(owned, mode='drop')

def reference(owned_x, owned_y, patch_dest):
    slab_x = place_blocks(owned_x, patch_dest).reshape(ROWS, K)
    slab_y = place_blocks(owned_y, patch_dest).reshape(ROWS, K)
    gram_mean = lax.dot_general(slab_x.astype(jnp.float32), slab_x.astype(jnp.float32), (((0,), (0,)), ((), ())), preferred_element_type=jnp.float32) / ROWS
    lower = jnp.linalg.cholesky(gram_mean)
    identity = jnp.eye(K, dtype=lower.dtype)
    inverse = lax.linalg.triangular_solve(lower, identity, left_side=True, lower=True)
    basis_rows = jnp.dot(slab_x.astype(jnp.float32), inverse.T, precision=lax.Precision.HIGHEST)
    projection = lax.dot_general(basis_rows, slab_y.astype(jnp.float32), (((0,), (0,)), ((), ())), precision=lax.Precision.HIGHEST) / math.sqrt(ROWS)
    return (basis_rows.reshape(ROW_BLOCKS, PATCH, K), lower.T, projection)
```

```python
import math

import jax
import jax.numpy as jnp
from jax import lax
from jax.sharding import PartitionSpec as P


from jax.experimental import pallas as pl
from jax.experimental.pallas import tpu as pltpu
HI = lax.Precision.HIGHEST

def small_inv(P, b):
    if b == 1:
        return [[1.0 / P[0][0]]]
    if b == 2:
        a, h, d = P[0][0], P[0][1], P[1][1]
        r = 1.0 / (a * d - h * h)
        return [[d * r, -h * r], [-h * r, a * r]]
    h = b // 2
    A = [[P[i][j] for j in range(h)] for i in range(h)]
    B = [[P[i][h + j] for j in range(h)] for i in range(h)]
    D = [[P[h + i][h + j] for j in range(h)] for i in range(h)]
    Ai = small_inv(A, h)
    AiB = [[sum(Ai[i][k] * B[k][j] for k in range(h)) for j in range(h)] for i in range(h)]
    S = [[None] * h for _ in range(h)]
    for i in range(h):
        for j in range(i, h):
            S[i][j] = D[i][j] - sum(B[k][i] * AiB[k][j] for k in range(h))
            S[j][i] = S[i][j]
    Si = small_inv(S, h)
    out = [[None] * b for _ in range(b)]
    BS = [[sum(AiB[i][k] * Si[k][j] for k in range(h)) for j in range(h)] for i in range(h)]
    for i in range(h):
        for j in range(h):
            out[h + i][h + j] = Si[i][j]
            out[i][h + j] = -BS[i][j]
            out[h + j][i] = -BS[i][j]
    for i in range(h):
        for j in range(i, h):
            v = Ai[i][j] + sum(BS[i][k] * AiB[j][k] for k in range(h))
            out[i][j] = v
            out[j][i] = v
    return out

def diag_block(D, b, r_out, w_out):
    lane = lax.broadcasted_iota(jnp.int32, (1, 128), 1)
    sub = lax.broadcasted_iota(jnp.int32, (8, 1), 0)
    M = list(D)
    for g in range(0, 128, b):
        v0, s0 = g // 8, g % 8
        r = [M[v0][s0 + s:s0 + s + 1, :] for s in range(b)]
        C0 = [jnp.broadcast_to(M[v0][:, g + t:g + t + 1], (8, 128)) for t in range(b)]
        P = [[C0[t][s0 + s:s0 + s + 1, :] for t in range(b)] for s in range(b)]
        ingroup = (lane >= g) & (lane < g + b)
        rp = [jnp.where(ingroup, jnp.where(lane == g + s, 1.0, 0.0), r[s]) for s in range(b)]
        if g + b < 128:
            Pi = small_inv(P, b)
            rt = [sum(Pi[s][t] * rp[t] for t in range(b)) for s in range(b)]
            for v in range(v0, 16):
                if v == v0 and s0 + b >= 8:
                    continue
                new = jnp.where(ingroup, 0.0, M[v])
                for s in range(b):
                    cs = C0[s] if v == v0 else M[v][:, g + s:g + s + 1]
                    new = new - cs * rt[s]
                if v == v0:
                    new = jnp.where(sub >= s0 + b, new, M[v])
                M[v] = new
        er, eb = list(r), list(rp)
        p = [list(row) for row in P]
        for s in range(b):
            sc = lax.rsqrt(p[s][s])
            for t in range(s + 1, b):
                m = p[s][t] / p[s][s]
                er[t] = er[t] - m * er[s]
                eb[t] = eb[t] - m * eb[s]
                for q in range(t, b):
                    p[t][q] = p[t][q] - m * p[s][q]
            r_out[g + s:g + s + 1, :] = jnp.where(lane >= g + s, er[s] * sc, 0.0)
            w_out[g + s:g + s + 1, :] = jnp.where(lane <= g + s, eb[s] * sc, 0.0)

def factor(M, R, W, wk, rk, nblk=4, b=4):
    n = nblk * 128
    colb = lax.broadcasted_iota(jnp.int32, (1, n), 1) // 128
    def outer(k, _):
        o = pl.multiple_of(k * 128, 128)
        kb = pl.ds(o, 128)
        D = [M[pl.ds(pl.multiple_of(o + 8 * v, 8), 8), kb] for v in range(16)]
        diag_block(D, b, rk, wk)
        M[kb, kb] = (lax.broadcasted_iota(jnp.int32, (128, 128), 0) == lax.broadcasted_iota(jnp.int32, (128, 128), 1)).astype(jnp.float32)
        row = jnp.dot(wk[...], M[kb, :], precision=HI, preferred_element_type=jnp.float32)
        M[kb, :] = row
        W[kb, :] = jnp.where(colb <= k, row, 0.0)
        R[kb, :] = jnp.where(colb > k, row, 0.0)
        R[kb, kb] = rk[...]
        def trail(i, _):
            ib = pl.ds(pl.multiple_of(i * 128, 128), 128)
            lik = M[kb, ib]
            upd = lax.dot_general(lik, M[kb, :], (((0,), (0,)), ((), ())), precision=HI, preferred_element_type=jnp.float32)
            M[ib, :] = jnp.where(colb == k, 0.0, M[ib, :]) - upd
            return 0
        lax.fori_loop(k + 1, nblk, trail, 0)
        return 0
    lax.fori_loop(0, nblk, outer, 0)


PATCH = 128
BLK_DEV = 64


def in_order(pieces, dim):
    pieces = jnp.moveaxis(pieces, 0, dim)
    shape = pieces.shape
    return pieces.reshape(*shape[:dim], shape[dim] * shape[dim + 1], *shape[dim + 2 :])


def from_everyone(array, axis):
    copies = jnp.broadcast_to(array, (lax.axis_size(axis), *array.shape))
    return lax.all_to_all(copies, axis, split_axis=0, concat_axis=0, tiled=True)


def collect(array, axis, dim):
    return in_order(from_everyone(array, axis), dim)


def slab_ranks(destination, per_slab):
    target = jnp.where(destination >= 0, destination // per_slab, -1)
    slot_count = destination.shape[-1]
    same_slab = target[..., :, None] == target[..., None, :]
    before = lax.broadcasted_iota(jnp.int32, (slot_count, slot_count), 1) < lax.broadcasted_iota(
        jnp.int32, (slot_count, slot_count), 0
    )
    order_rank = jnp.sum((same_slab & before).astype(jnp.int32), axis=-1)
    return (target, order_rank)


def send_table(destination, per_slab, slab_count, capacity):
    target, order_rank = slab_ranks(destination, per_slab)
    slot_count = destination.shape[0]
    where_to = jnp.where(target >= 0, target * capacity + order_rank, slab_count * capacity)
    start_table = jnp.full((slab_count * capacity,), slot_count, jnp.int32)
    return start_table.at[where_to].set(jnp.arange(slot_count, dtype=jnp.int32), mode="drop")


def arrival_index(all_lists, per_slab, capacity, my_slab):
    slot_count = all_lists.shape[1]
    target, order_rank = slab_ranks(all_lists, per_slab)
    wanted = my_slab * per_slab + jnp.arange(per_slab, dtype=jnp.int32)
    matches = all_lists.reshape(-1)[None, :] == wanted[:, None]
    located = jnp.argmax(matches, axis=1)
    source = located // slot_count
    return source * capacity + order_rank.reshape(-1)[located]


def pick_rows(payload, indices):
    return jnp.take(payload, indices, axis=0, mode="fill", fill_value=0)


def factor_kernel(g, R, W, M, wk, rk):
    M[...] = g[...]
    factor(M, R, W, wk, rk)


def factor_call(g):
    S = jax.ShapeDtypeStruct((512, 512), jnp.float32)
    V = pl.BlockSpec(memory_space=pltpu.VMEM)
    small = pltpu.VMEM((128, 128), jnp.float32)
    return pl.pallas_call(
        factor_kernel,
        out_shape=(S, S),
        in_specs=[V],
        out_specs=(V, V),
        scratch_shapes=[pltpu.VMEM((512, 512), jnp.float32), small, small],
    )(g)


def body(owned_x, owned_y, patch_dest):
    slab_count = lax.axis_size("space")
    slot_count = patch_dest.shape[0]
    capacity = slot_count // slab_count
    my_slab = lax.axis_index("space")
    all_lists = collect(patch_dest, "space", 0)
    outgoing_table = send_table(patch_dest, BLK_DEV, slab_count, capacity)
    received_at = arrival_index(
        all_lists.reshape(slab_count, slot_count), BLK_DEV, capacity, my_slab
    )
    rows_total = slab_count * BLK_DEV * PATCH
    contract = (((0,), (0,)), ((), ()))
    block_x, block_y = (
        lax.all_to_all(owned_x, "snap", split_axis=1, concat_axis=2, tiled=True),
        lax.all_to_all(owned_y, "snap", split_axis=1, concat_axis=2, tiled=True),
    )
    width = block_x.shape[-1]
    used = patch_dest >= 0
    kept_x = jnp.where(used[:, None, None], block_x, jnp.zeros_like(block_x))
    local_cross = lax.dot_general(
        kept_x.reshape(-1, width),
        block_y.reshape(-1, width),
        contract,
        preferred_element_type=jnp.float32,
    )
    moved_x = lax.all_to_all(
        pick_rows(block_x, outgoing_table), "space", split_axis=0, concat_axis=0, tiled=True
    )
    slab_x = jnp.take(moved_x, received_at, axis=0)
    cell_rows = slab_x.reshape(-1, width)
    local_gram = lax.dot_general(cell_rows, cell_rows, contract, preferred_element_type=jnp.float32)
    gram_total, cross_total = lax.psum((local_gram, local_cross), ("space", "snap"))
    upper, inverse = factor_call(gram_total / rows_total)
    basis_rows = jnp.dot(cell_rows.astype(jnp.float32), inverse.T, precision=lax.Precision.HIGHEST)
    projection = jnp.dot(inverse, cross_total, precision=lax.Precision.HIGHEST) / math.sqrt(
        rows_total
    )
    return (basis_rows.reshape(slab_x.shape[0], slab_x.shape[1], width), upper, projection)


def solution(mesh):
    in_specs = (P("space", None, "snap"), P("space", None, "snap"), P("space"))
    out_specs = (P("space", "snap", None), P(), P())
    return jax.shard_map(body, mesh=mesh, in_specs=in_specs, out_specs=out_specs, check_vma=False)
```

```python
import jax
import jax.numpy as jnp
from jax import lax
from jax.experimental import pallas as pl
from jax.experimental.pallas import tpu as pltpu
from jax.sharding import PartitionSpec as P

BLK_DEV = 64
HI = lax.Precision.HIGHEST

def small_inv(P, b):
    if b == 1:
        return [[1.0 / P[0][0]]]
    if b == 2:
        a, h, d = P[0][0], P[0][1], P[1][1]
        r = 1.0 / (a * d - h * h)
        return [[d * r, -h * r], [-h * r, a * r]]
    h = b // 2
    A = [[P[i][j] for j in range(h)] for i in range(h)]
    B = [[P[i][h + j] for j in range(h)] for i in range(h)]
    D = [[P[h + i][h + j] for j in range(h)] for i in range(h)]
    Ai = small_inv(A, h)
    AiB = [[sum(Ai[i][k] * B[k][j] for k in range(h)) for j in range(h)] for i in range(h)]
    S = [[None] * h for _ in range(h)]
    for i in range(h):
        for j in range(i, h):
            S[i][j] = D[i][j] - sum(B[k][i] * AiB[k][j] for k in range(h))
            S[j][i] = S[i][j]
    Si = small_inv(S, h)
    out = [[None] * b for _ in range(b)]
    BS = [[sum(AiB[i][k] * Si[k][j] for k in range(h)) for j in range(h)] for i in range(h)]
    for i in range(h):
        for j in range(h):
            out[h + i][h + j] = Si[i][j]
            out[i][h + j] = -BS[i][j]
            out[h + j][i] = -BS[i][j]
    for i in range(h):
        for j in range(i, h):
            v = Ai[i][j] + sum(BS[i][k] * AiB[j][k] for k in range(h))
            out[i][j] = v
            out[j][i] = v
    return out

def diag_block(D, b, r_out, w_out):
    lane = lax.broadcasted_iota(jnp.int32, (1, 128), 1)
    sub = lax.broadcasted_iota(jnp.int32, (8, 1), 0)
    M = list(D)
    for g in range(0, 128, b):
        v0, s0 = g // 8, g % 8
        r = [M[v0][s0 + s:s0 + s + 1, :] for s in range(b)]
        C0 = [jnp.broadcast_to(M[v0][:, g + t:g + t + 1], (8, 128)) for t in range(b)]
        P = [[C0[t][s0 + s:s0 + s + 1, :] for t in range(b)] for s in range(b)]
        ingroup = (lane >= g) & (lane < g + b)
        rp = [jnp.where(ingroup, jnp.where(lane == g + s, 1.0, 0.0), r[s]) for s in range(b)]
        if g + b < 128:
            Pi = small_inv(P, b)
            rt = [sum(Pi[s][t] * rp[t] for t in range(b)) for s in range(b)]
            for v in range(v0, 16):
                if v == v0 and s0 + b >= 8:
                    continue
                new = jnp.where(ingroup, 0.0, M[v])
                for s in range(b):
                    cs = C0[s] if v == v0 else M[v][:, g + s:g + s + 1]
                    new = new - cs * rt[s]
                if v == v0:
                    new = jnp.where(sub >= s0 + b, new, M[v])
                M[v] = new
        er, eb = list(r), list(rp)
        p = [list(row) for row in P]
        for s in range(b):
            sc = lax.rsqrt(p[s][s])
            for t in range(s + 1, b):
                m = p[s][t] / p[s][s]
                er[t] = er[t] - m * er[s]
                eb[t] = eb[t] - m * eb[s]
                for q in range(t, b):
                    p[t][q] = p[t][q] - m * p[s][q]
            r_out[g + s:g + s + 1, :] = jnp.where(lane >= g + s, er[s] * sc, 0.0)
            w_out[g + s:g + s + 1, :] = jnp.where(lane <= g + s, eb[s] * sc, 0.0)

def factor(M, R, W, wk, rk, nblk=4, b=4):
    n = nblk * 128
    colb = lax.broadcasted_iota(jnp.int32, (1, n), 1) // 128
    def outer(k, _):
        o = pl.multiple_of(k * 128, 128)
        kb = pl.ds(o, 128)
        D = [M[pl.ds(pl.multiple_of(o + 8 * v, 8), 8), kb] for v in range(16)]
        diag_block(D, b, rk, wk)
        M[kb, kb] = (lax.broadcasted_iota(jnp.int32, (128, 128), 0) == lax.broadcasted_iota(jnp.int32, (128, 128), 1)).astype(jnp.float32)
        row = jnp.dot(wk[...], M[kb, :], precision=HI, preferred_element_type=jnp.float32)
        M[kb, :] = row
        W[kb, :] = jnp.where(colb <= k, row, 0.0)
        R[kb, :] = jnp.where(colb > k, row, 0.0)
        R[kb, kb] = rk[...]
        def trail(i, _):
            ib = pl.ds(pl.multiple_of(i * 128, 128), 128)
            lik = M[kb, ib]
            upd = lax.dot_general(lik, M[kb, :], (((0,), (0,)), ((), ())), precision=HI, preferred_element_type=jnp.float32)
            M[ib, :] = jnp.where(colb == k, 0.0, M[ib, :]) - upd
            return 0
        lax.fori_loop(k + 1, nblk, trail, 0)
        return 0
    lax.fori_loop(0, nblk, outer, 0)


ROWS = 262144
MESH = pl.DeviceIdType.MESH
F32 = jnp.float32
BF16 = jnp.bfloat16
ORDER = (0, 2, 1, 3)
CHUNKS = 8
GT = 160
CT = 256


def where_am_i():
    s = lax.axis_index("space")
    return s // 8, (s // 2) % 4, s % 2, lax.axis_index("snap"), s


def space_of(y, x, c):
    return (lax.rem(y, 4) * 4 + lax.rem(x, 4)) * 2 + lax.rem(c, 2)


def remote(src, dst, ss, rs, space=None, snap=None):
    dev = {}
    if space is not None:
        dev["space"] = space
    if snap is not None:
        dev["snap"] = snap
    return pltpu.make_async_remote_copy(
        src_ref=src, dst_ref=dst, send_sem=ss, recv_sem=rs, device_id=dev, device_id_type=MESH
    )


def loop(lo, hi, body):
    def step(i, carry):
        body(i)
        return carry

    lax.fori_loop(lo, hi, step, 0)


def column(row):
    eye = lax.broadcasted_iota(jnp.int32, (128, 128), 0) == lax.broadcasted_iota(jnp.int32, (128, 128), 1)
    return jnp.sum(jnp.where(eye, jnp.broadcast_to(row, (128, 128)), 0), axis=1, keepdims=True)


def slot_tables(dest, y, x, c):
    slab = jnp.where(dest >= 0, dest // BLK_DEV, -1)
    lane = lax.broadcasted_iota(jnp.int32, (128, 128), 1)
    sub = lax.broadcasted_iota(jnp.int32, (128, 128), 0)
    same = (column(slab) == slab) & (sub < lane)
    rank = jnp.sum(same.astype(jnp.int32), axis=0, keepdims=True)
    dy = (slab // 8 - y + 4) % 4
    dx = ((slab // 2) % 4 - x + 4) % 4
    dc = (slab % 2 - c + 2) % 2
    place = jnp.where(dy == 1, 2, jnp.where(dy == 2, 1, dy))
    pos = ((dc * 4 + (dx - dy + 4) % 4) * 4 + place) * 4 + rank
    pos = column(jnp.where(dest >= 0, pos, -1))
    hit = pos == lane
    slot = jnp.sum(jnp.where(hit, sub - 128, 0), axis=0, keepdims=True) + 128
    block = jnp.sum(jnp.where(hit, column(dest) + 1, 0), axis=0, keepdims=True) - 1
    return slot, block


def all_sum(n, tiles, b1, half, b2, piece, zb, half2, full, s1, r1, s2, r2, s3, r3, s4, r4, s5, r5, after_z=None):
    y, x, c, z, s = where_am_i()
    chip = s // 2
    h, m = n // 2, n // 32
    mate = chip * 2 + (1 - c)
    cp1 = remote(tiles.at[pl.ds((1 - c) * h, h)], b1, s1.at[0], r1.at[0], space=mate)
    cp1.start()
    cp1.wait_recv()
    half[...] = tiles[pl.ds(c * h, h)] + b1[...]

    def chip_at(d):
        return lax.rem(y + d // 4, 4) * 4 + lax.rem(x + lax.rem(d, 4), 4)

    def scatter(d):
        q = chip_at(d)
        return remote(half.at[pl.ds(q * m, m)], b2.at[chip], s2.at[d], r2.at[d], space=q * 2 + c)

    loop(1, 16, lambda d: scatter(d).start())
    b2[chip] = half[pl.ds(chip * m, m)]
    loop(1, 16, lambda d: scatter(d).wait_recv())
    total = b2[0]
    for q in range(1, 16):
        total = total + b2[q]
    piece[...] = total
    zcp = [remote(piece, zb.at[z], s3.at[d - 1], r3.at[d - 1], snap=lax.rem(z + d, 4)) for d in (1, 2, 3)]
    for cp in zcp:
        cp.start()
    if after_z is not None:
        after_z()
    zb[z] = piece[...]
    for cp in zcp:
        cp.wait_recv()
    half2[pl.ds(chip * m, m)] = zb[0] + zb[1] + zb[2] + zb[3]

    def gather(d):
        mine = pl.ds(chip * m, m)
        return remote(half2.at[mine], half2.at[mine], s4.at[d], r4.at[d], space=chip_at(d) * 2 + c)

    loop(1, 16, lambda d: gather(d).start())
    loop(1, 16, lambda d: gather(d).wait_recv())
    cp5 = remote(half2, full.at[pl.ds(c * h, h)], s5.at[0], r5.at[0], space=mate)
    cp5.start()
    full[pl.ds(c * h, h)] = half2[...]
    cp5.wait_recv()

    def drain():
        cp1.wait_send()
        loop(1, 16, lambda d: scatter(d).wait_send())
        for cp in zcp:
            cp.wait_send()
        loop(1, 16, lambda d: gather(d).wait_send())
        cp5.wait_send()

    return drain


def sum_scratch(n):
    h, m = n // 2, n // 32
    dma = pltpu.SemaphoreType.DMA
    return [
        pltpu.VMEM((n, 8, 128), F32),
        pltpu.VMEM((h, 8, 128), F32),
        pltpu.VMEM((h, 8, 128), F32),
        pltpu.VMEM((16, m, 8, 128), F32),
        pltpu.VMEM((m, 8, 128), F32),
        pltpu.VMEM((4, m, 8, 128), F32),
        pltpu.VMEM((h, 8, 128), F32),
        pltpu.VMEM((n, 8, 128), F32),
        dma((1,)), dma((1,)), dma((16,)), dma((16,)), dma((3,)), dma((3,)), dma((16,)), dma((16,)), dma((1,)), dma((1,)),
    ]


def whole(dest, x_hbm, y_hbm, q_hbm, r_out, p_out, xin, yin, xo, yo, xr, yr, sr, xs, qv, acc, M, W, wk, rk,
          ids, tab_v, tab_s, at_v, at_s, lsem, tsem, qsem, xs_s, xs_r, ys_s, ys_r, sp_s, sp_r, id_s, id_r, *sums):
    y, x, c, z, s = where_am_i()
    gsum, csum = sums[:18], sums[18:]
    load_x = pltpu.make_async_copy(x_hbm, xin.at[pl.ds(0, 128)], lsem.at[0])
    load_y = pltpu.make_async_copy(y_hbm, yin.at[pl.ds(0, 128)], lsem.at[1])
    load_x.start()
    load_y.start()

    def space_at(k, j):
        a = ORDER[j]
        return space_of(y + a, x + a + lax.rem(k, 4), c + k // 4)

    barrier = pltpu.get_barrier_semaphore()
    for o in range(1, 32):
        pl.semaphore_signal(barrier, inc=1, device_id={"space": space_at(o // 4, o % 4)}, device_id_type=MESH)
    for d in (1, 2, 3):
        pl.semaphore_signal(barrier, inc=1, device_id={"snap": lax.rem(z + d, 4)}, device_id_type=MESH)

    xin[128] = jnp.zeros((128, 128), BF16)
    yin[128] = jnp.zeros((128, 128), BF16)
    slot, block = slot_tables(dest[...], y, x, c)
    tab_v[...] = jnp.broadcast_to(jnp.clip(slot, 0, 128), (8, 128))
    ids[s] = jnp.broadcast_to(block, (8, 128))
    tab_copy = pltpu.make_async_copy(tab_v, tab_s, tsem.at[0])
    tab_copy.start()
    tab_copy.wait()
    load_x.wait()

    def order_slots(src, dst, recv, k):
        def one(i):
            got = src[tab_s[0, i]]
            for q in range(4):
                dst[q, i] = got[32 * q:32 * q + 32]
            recv[z, i] = dst[z, i]

        loop(16 * k, 16 * k + 16, one)

    def over_z(src, recv, ss, rs, k):
        span = pl.ds(16 * k, 16)
        out = []
        for d in (1, 2, 3):
            to = lax.rem(z + d, 4)
            out.append(remote(src.at[to, span], recv.at[z, span], ss.at[k, d - 1], rs.at[k, d - 1], snap=to))
        return out

    def send_z(src, recv, ss, rs, k):
        for cp in over_z(src, recv, ss, rs, k):
            cp.start()

    order_slots(xin, xo, xr, 0)
    pl.semaphore_wait(barrier, 34)
    for k in range(1, CHUNKS):
        order_slots(xin, xo, xr, k)
        send_z(xo, xr, xs_s, xs_r, k - 1)
    load_y.wait()
    order_slots(yin, yo, yr, 0)
    send_z(xo, xr, xs_s, xs_r, CHUNKS - 1)

    def send_ids(k, j):
        o = 4 * k + j
        return remote(ids.at[s], ids.at[s], id_s.at[o], id_r.at[o], space=space_at(k, j))

    for o in range(1, 32):
        send_ids(o // 4, o % 4).start()
    loop(1, CHUNKS, lambda k: order_slots(yin, yo, yr, k))
    send_z(yo, yr, ys_s, ys_r, 0)

    for o in range(1, 32):
        send_ids(o // 4, o % 4).wait_recv()
    wanted = s * BLK_DEV + lax.broadcasted_iota(jnp.int32, (BLK_DEV, 1), 0)
    place = lax.rem(lax.broadcasted_iota(jnp.int32, (1, 128), 1), 4)
    found = jnp.zeros((BLK_DEV, 128), jnp.int32)
    for src in range(32):
        found = found + jnp.where(ids[src][0:1, :] == wanted, place + 4 * src, 0)
    found = jnp.sum(found, axis=1, keepdims=True)
    pick = lax.broadcasted_iota(jnp.int32, (BLK_DEV, 128), 0) == lax.broadcasted_iota(jnp.int32, (BLK_DEV, 128), 1)
    found = jnp.sum(jnp.where(pick, found, 0), axis=0, keepdims=True)
    at_v[...] = jnp.broadcast_to(jnp.clip(found, 0, 127), (8, 128))
    at_copy = pltpu.make_async_copy(at_v, at_s, tsem.at[1])
    at_copy.start()
    at_copy.wait()

    def to_slab(k, j):
        o = 4 * k + j
        return remote(xr.at[:, pl.ds(4 * o, 4)], sr.at[:, pl.ds(4 * s, 4)], sp_s.at[o], sp_r.at[o], space=space_at(k, j))

    def panel_rows(buf, k):
        return jnp.concatenate([buf[p, pl.ds(16 * k, 16)].reshape(512, 128) for p in range(4)], axis=1)

    acc[...] = jnp.zeros((512, 512), F32)
    contract = (((0,), (0,)), ((), ()))

    def gram_step(k):
        for cp in over_z(xo, xr, xs_s, xs_r, k):
            cp.wait_recv()
        for j in range(4):
            if j == 0:
                @pl.when(k > 0)
                def _():
                    to_slab(k, 0).start()

                @pl.when(k == 0)
                def _():
                    sr[:, pl.ds(4 * s, 4)] = xr[:, 0:4]
            else:
                to_slab(k, j).start()
        rows = panel_rows(xr, k)
        acc[...] += lax.dot_general(rows, rows, contract, preferred_element_type=F32)

    loop(0, CHUNKS, gram_step)

    def later_y():
        for k in range(1, CHUNKS):
            send_z(yo, yr, ys_s, ys_r, k)

    b = 0
    for i in range(4):
        for j in range(i, 4):
            gsum[0][16 * b:16 * b + 16] = acc[128 * i:128 * i + 128, 128 * j:128 * j + 128].reshape(16, 8, 128)
            b += 1
    drain_g = all_sum(GT, *gsum, after_z=later_y)
    full = gsum[7]
    b = 0
    for i in range(4):
        for j in range(i, 4):
            M[128 * i:128 * i + 128, 128 * j:128 * j + 128] = full[16 * b:16 * b + 16].reshape(128, 128) * (1.0 / ROWS)
            b += 1
    factor(M, r_out, W, wk, rk)

    for o in range(1, 32):
        to_slab(o // 4, o % 4).wait_recv()

    def pick_block(i):
        at = at_s[0, i]
        for p in range(4):
            xs[i, :, 128 * p:128 * p + 128] = sr[p, at]

    loop(0, BLK_DEV, pick_block)
    w1 = W[...].astype(BF16)
    w2 = (W[...] - w1.astype(F32)).astype(BF16)
    w3 = (W[...] - w1.astype(F32) - w2.astype(F32)).astype(BF16)
    last = (((1,), (1,)), ((), ()))

    def store_q(i):
        span = pl.ds(16 * i, 16)
        return pltpu.make_async_copy(qv.at[span], q_hbm.at[span], qsem.at[i])

    def basis(i):
        span = pl.ds(16 * i, 16)
        rows = xs[span].reshape(512, 512)
        out = lax.dot_general(rows, w3, last, preferred_element_type=F32)
        out = out + lax.dot_general(rows, w2, last, preferred_element_type=F32)
        out = out + lax.dot_general(rows, w1, last, preferred_element_type=F32)
        qv[span] = out.reshape(16, 32, 512)
        store_q(i).start()

    loop(0, 4, basis)

    acc[...] = jnp.zeros((512, 512), F32)

    def cross_step(k):
        for cp in over_z(yo, yr, ys_s, ys_r, k):
            cp.wait_recv()
        acc[...] += lax.dot_general(panel_rows(xr, k), panel_rows(yr, k), contract, preferred_element_type=F32)

    loop(0, CHUNKS, cross_step)
    for j in range(4):
        csum[0][64 * j:64 * j + 64] = acc[:, 128 * j:128 * j + 128].reshape(64, 8, 128)
    drain_c = all_sum(CT, *csum)
    for j in range(4):
        M[:, 128 * j:128 * j + 128] = csum[7][64 * j:64 * j + 64].reshape(512, 128)
    p_out[...] = jnp.dot(W[...], M[...], precision=HI, preferred_element_type=F32) * (1.0 / 512.0)

    loop(0, 4, lambda i: store_q(i).wait())
    drain_g()
    drain_c()
    for o in range(1, 32):
        send_ids(o // 4, o % 4).wait_send()
        to_slab(o // 4, o % 4).wait_send()

    def drain_z(k):
        for cp in over_z(xo, xr, xs_s, xs_r, k) + over_z(yo, yr, ys_s, ys_r, k):
            cp.wait_send()

    loop(0, CHUNKS, drain_z)


def body(owned_x, owned_y, patch_dest):
    V = pl.BlockSpec(memory_space=pltpu.VMEM)
    A = pl.BlockSpec(memory_space=pl.ANY)
    dma = pltpu.SemaphoreType.DMA
    square = jax.ShapeDtypeStruct((512, 512), F32)
    panels = pltpu.VMEM((4, 128, 32, 128), BF16)
    return pl.pallas_call(
        whole,
        out_shape=(jax.ShapeDtypeStruct((BLK_DEV, 32, 512), F32), square, square),
        in_specs=[V, A, A],
        out_specs=(A, V, V),
        scratch_shapes=[
            pltpu.VMEM((129, 128, 128), BF16),
            pltpu.VMEM((129, 128, 128), BF16),
            panels, panels, panels, panels, panels,
            pltpu.VMEM((BLK_DEV, 32, 512), BF16),
            pltpu.VMEM((BLK_DEV, 32, 512), F32),
            pltpu.VMEM((512, 512), F32),
            pltpu.VMEM((512, 512), F32),
            pltpu.VMEM((512, 512), F32),
            pltpu.VMEM((128, 128), F32),
            pltpu.VMEM((128, 128), F32),
            pltpu.VMEM((32, 8, 128), jnp.int32),
            pltpu.VMEM((8, 128), jnp.int32),
            pltpu.SMEM((8, 128), jnp.int32),
            pltpu.VMEM((8, 128), jnp.int32),
            pltpu.SMEM((8, 128), jnp.int32),
            dma((2,)), dma((2,)), dma((4,)),
            dma((CHUNKS, 3)), dma((CHUNKS, 3)), dma((CHUNKS, 3)), dma((CHUNKS, 3)),
            dma((32,)), dma((32,)), dma((32,)), dma((32,)),
        ] + sum_scratch(GT) + sum_scratch(CT),
        compiler_params=pltpu.CompilerParams(
            collective_id=0, has_side_effects=True, vmem_limit_bytes=63 << 20
        ),
        name="window",
    )(patch_dest.reshape(1, 128), owned_x, owned_y)


def solution(mesh):
    in_specs = (P("space", None, "snap"), P("space", None, "snap"), P("space"))
    out_specs = (P("space", "snap", None), P(), P())
    return jax.shard_map(body, mesh=mesh, in_specs=in_specs, out_specs=out_specs, check_vma=False)
```

```python
import jax
import jax.numpy as jnp
from jax import lax
from jax.experimental import pallas as pl
from jax.experimental.pallas import tpu as pltpu
from jax.sharding import PartitionSpec as P

BLK_DEV = 64
HI = lax.Precision.HIGHEST

def small_inv(P, b):
    if b == 1:
        return [[1.0 / P[0][0]]]
    if b == 2:
        a, h, d = P[0][0], P[0][1], P[1][1]
        r = 1.0 / (a * d - h * h)
        return [[d * r, -h * r], [-h * r, a * r]]
    h = b // 2
    A = [[P[i][j] for j in range(h)] for i in range(h)]
    B = [[P[i][h + j] for j in range(h)] for i in range(h)]
    D = [[P[h + i][h + j] for j in range(h)] for i in range(h)]
    Ai = small_inv(A, h)
    AiB = [[sum(Ai[i][k] * B[k][j] for k in range(h)) for j in range(h)] for i in range(h)]
    S = [[None] * h for _ in range(h)]
    for i in range(h):
        for j in range(i, h):
            S[i][j] = D[i][j] - sum(B[k][i] * AiB[k][j] for k in range(h))
            S[j][i] = S[i][j]
    Si = small_inv(S, h)
    out = [[None] * b for _ in range(b)]
    BS = [[sum(AiB[i][k] * Si[k][j] for k in range(h)) for j in range(h)] for i in range(h)]
    for i in range(h):
        for j in range(h):
            out[h + i][h + j] = Si[i][j]
            out[i][h + j] = -BS[i][j]
            out[h + j][i] = -BS[i][j]
    for i in range(h):
        for j in range(i, h):
            v = Ai[i][j] + sum(BS[i][k] * AiB[j][k] for k in range(h))
            out[i][j] = v
            out[j][i] = v
    return out

def diag_block(D, b, r_out, w_out):
    lane = lax.broadcasted_iota(jnp.int32, (1, 128), 1)
    sub = lax.broadcasted_iota(jnp.int32, (8, 1), 0)
    M = list(D)
    for g in range(0, 128, b):
        v0, s0 = g // 8, g % 8
        r = [M[v0][s0 + s:s0 + s + 1, :] for s in range(b)]
        C0 = [jnp.broadcast_to(M[v0][:, g + t:g + t + 1], (8, 128)) for t in range(b)]
        P = [[C0[t][s0 + s:s0 + s + 1, :] for t in range(b)] for s in range(b)]
        ingroup = (lane >= g) & (lane < g + b)
        rp = [jnp.where(ingroup, jnp.where(lane == g + s, 1.0, 0.0), r[s]) for s in range(b)]
        if g + b < 128:
            Pi = small_inv(P, b)
            rt = [sum(Pi[s][t] * rp[t] for t in range(b)) for s in range(b)]
            for v in range(v0, 16):
                if v == v0 and s0 + b >= 8:
                    continue
                new = jnp.where(ingroup, 0.0, M[v])
                for s in range(b):
                    cs = C0[s] if v == v0 else M[v][:, g + s:g + s + 1]
                    new = new - cs * rt[s]
                if v == v0:
                    new = jnp.where(sub >= s0 + b, new, M[v])
                M[v] = new
        er, eb = list(r), list(rp)
        p = [list(row) for row in P]
        for s in range(b):
            sc = lax.rsqrt(p[s][s])
            for t in range(s + 1, b):
                m = p[s][t] / p[s][s]
                er[t] = er[t] - m * er[s]
                eb[t] = eb[t] - m * eb[s]
                for q in range(t, b):
                    p[t][q] = p[t][q] - m * p[s][q]
            r_out[g + s:g + s + 1, :] = jnp.where(lane >= g + s, er[s] * sc, 0.0)
            w_out[g + s:g + s + 1, :] = jnp.where(lane <= g + s, eb[s] * sc, 0.0)

def factor(M, R, W, wk, rk, nblk=4, b=4):
    n = nblk * 128
    colb = lax.broadcasted_iota(jnp.int32, (1, n), 1) // 128
    def outer(k, _):
        o = pl.multiple_of(k * 128, 128)
        kb = pl.ds(o, 128)
        D = [M[pl.ds(pl.multiple_of(o + 8 * v, 8), 8), kb] for v in range(16)]
        diag_block(D, b, rk, wk)
        M[kb, kb] = (lax.broadcasted_iota(jnp.int32, (128, 128), 0) == lax.broadcasted_iota(jnp.int32, (128, 128), 1)).astype(jnp.float32)
        row = jnp.dot(wk[...], M[kb, :], precision=HI, preferred_element_type=jnp.float32)
        M[kb, :] = row
        W[kb, :] = jnp.where(colb <= k, row, 0.0)
        R[kb, :] = jnp.where(colb > k, row, 0.0)
        R[kb, kb] = rk[...]
        def trail(i, _):
            ib = pl.ds(pl.multiple_of(i * 128, 128), 128)
            lik = M[kb, ib]
            upd = lax.dot_general(lik, M[kb, :], (((0,), (0,)), ((), ())), precision=HI, preferred_element_type=jnp.float32)
            M[ib, :] = jnp.where(colb == k, 0.0, M[ib, :]) - upd
            return 0
        lax.fori_loop(k + 1, nblk, trail, 0)
        return 0
    lax.fori_loop(0, nblk, outer, 0)


ROWS = 262144
MESH = pl.DeviceIdType.MESH
F32 = jnp.float32
BF16 = jnp.bfloat16
ORDER = (0, 2, 1, 3)
CHUNKS = 8
EARLY = 5
FIRST_Y = 2
CT = 256
G_GROUPS = ((0, 64), (64, 96))
C_GROUPS = ((0, 64), (64, 64), (128, 64), (192, 64))


def where_am_i():
    s = lax.axis_index("space")
    return s // 8, (s // 2) % 4, s % 2, lax.axis_index("snap"), s


def space_of(y, x, c):
    return (lax.rem(y, 4) * 4 + lax.rem(x, 4)) * 2 + lax.rem(c, 2)


def remote(src, dst, ss, rs, space=None, snap=None):
    dev = {}
    if space is not None:
        dev["space"] = space
    if snap is not None:
        dev["snap"] = snap
    return pltpu.make_async_remote_copy(
        src_ref=src, dst_ref=dst, send_sem=ss, recv_sem=rs, device_id=dev, device_id_type=MESH
    )


def loop(lo, hi, body):
    def step(i, carry):
        body(i)
        return carry

    lax.fori_loop(lo, hi, step, 0)


def column(row):
    eye = lax.broadcasted_iota(jnp.int32, (128, 128), 0) == lax.broadcasted_iota(jnp.int32, (128, 128), 1)
    return jnp.sum(jnp.where(eye, jnp.broadcast_to(row, (128, 128)), 0), axis=1, keepdims=True)


def slot_tables(dest, y, x, c):
    slab = jnp.where(dest >= 0, dest // BLK_DEV, -1)
    lane = lax.broadcasted_iota(jnp.int32, (128, 128), 1)
    sub = lax.broadcasted_iota(jnp.int32, (128, 128), 0)
    same = (column(slab) == slab) & (sub < lane)
    rank = jnp.sum(same.astype(jnp.int32), axis=0, keepdims=True)
    dy = (slab // 8 - y + 4) % 4
    dx = ((slab // 2) % 4 - x + 4) % 4
    dc = (slab % 2 - c + 2) % 2
    place = jnp.where(dy == 1, 2, jnp.where(dy == 2, 1, dy))
    pos = ((dc * 4 + (dx - dy + 4) % 4) * 4 + place) * 4 + rank
    pos = column(jnp.where(dest >= 0, pos, -1))
    hit = pos == lane
    slot = jnp.sum(jnp.where(hit, sub - 128, 0), axis=0, keepdims=True) + 128
    block = jnp.sum(jnp.where(hit, column(dest) + 1, 0), axis=0, keepdims=True) - 1
    return slot, block


def all_sum(groups, tiles, b1, half, b2, piece, zb, half2, full, s1, r1, s2, r2, s3, r3, s4, r4, s5, r5, after_scatter=None, after_z=None):
    y, x, c, z, s = where_am_i()
    chip = s // 2
    mate = chip * 2 + (1 - c)

    def chip_at(d):
        return lax.rem(y + d // 4, 4) * 4 + lax.rem(x + lax.rem(d, 4), 4)

    spans = [(g, at, n // 2, n // 32) for g, (at, n) in enumerate(groups)]

    def swap(g, at, h, m):
        return remote(tiles.at[pl.ds(at + (1 - c) * h, h)], b1.at[at // 2:at // 2 + h], s1.at[g], r1.at[g], space=mate)

    def scatter(g, at, h, m, d):
        q = chip_at(d)
        return remote(half.at[pl.ds(at // 2 + q * m, m)], b2.at[chip, at // 32:at // 32 + m], s2.at[g, d], r2.at[g, d], space=q * 2 + c)

    def across(g, at, h, m, d):
        mine = pl.ds(at // 32, m)
        return remote(piece.at[mine], zb.at[z, mine], s3.at[g, d], r3.at[g, d], snap=lax.rem(z + d, 4))

    def gather(g, at, h, m, d):
        mine = pl.ds(at // 2 + chip * m, m)
        return remote(half2.at[mine], half2.at[mine], s4.at[g, d], r4.at[g, d], space=chip_at(d) * 2 + c)

    def swap_back(g, at, h, m):
        return remote(half2.at[at // 2:at // 2 + h], full.at[pl.ds(at + c * h, h)], s5.at[g], r5.at[g], space=mate)

    for sp in spans:
        swap(*sp).start()
    for sp in spans:
        g, at, h, m = sp
        swap(*sp).wait_recv()
        half[at // 2:at // 2 + h] = tiles[pl.ds(at + c * h, h)] + b1[at // 2:at // 2 + h]
        loop(1, 16, lambda d: scatter(*sp, d).start())
        b2[chip, at // 32:at // 32 + m] = half[pl.ds(at // 2 + chip * m, m)]
    if after_scatter is not None:
        after_scatter()
    for sp in spans:
        g, at, h, m = sp
        loop(1, 16, lambda d: scatter(*sp, d).wait_recv())
        mine = slice(at // 32, at // 32 + m)
        total = b2[0, mine]
        for q in range(1, 16):
            total = total + b2[q, mine]
        piece[mine] = total
        for d in (1, 2, 3):
            across(*sp, d).start()
        zb[z, mine] = piece[mine]
    if after_z is not None:
        after_z()
    for sp in spans:
        g, at, h, m = sp
        for d in (1, 2, 3):
            across(*sp, d).wait_recv()
        mine = slice(at // 32, at // 32 + m)
        half2[pl.ds(at // 2 + chip * m, m)] = zb[0, mine] + zb[1, mine] + zb[2, mine] + zb[3, mine]
        loop(1, 16, lambda d: gather(*sp, d).start())
    for sp in spans:
        g, at, h, m = sp
        loop(1, 16, lambda d: gather(*sp, d).wait_recv())
        swap_back(*sp).start()
        full[pl.ds(at + c * h, h)] = half2[at // 2:at // 2 + h]
    for sp in spans:
        swap_back(*sp).wait_recv()

    def drain():
        for sp in spans:
            swap(*sp).wait_send()
            loop(1, 16, lambda d: scatter(*sp, d).wait_send())
            for d in (1, 2, 3):
                across(*sp, d).wait_send()
            loop(1, 16, lambda d: gather(*sp, d).wait_send())
            swap_back(*sp).wait_send()

    return drain


def sum_scratch(groups):
    n = sum(size for _, size in groups)
    k = len(groups)
    h, m = n // 2, n // 32
    dma = pltpu.SemaphoreType.DMA
    return [
        pltpu.VMEM((n, 8, 128), F32),
        pltpu.VMEM((h, 8, 128), F32),
        pltpu.VMEM((h, 8, 128), F32),
        pltpu.VMEM((16, m, 8, 128), F32),
        pltpu.VMEM((m, 8, 128), F32),
        pltpu.VMEM((4, m, 8, 128), F32),
        pltpu.VMEM((h, 8, 128), F32),
        pltpu.VMEM((n, 8, 128), F32),
        dma((k,)), dma((k,)), dma((k, 16)), dma((k, 16)), dma((k, 4)), dma((k, 4)), dma((k, 16)), dma((k, 16)), dma((k,)), dma((k,)),
    ]


def whole(dest, x_hbm, y_hbm, q_hbm, r_out, w_out, c_out, xin, yin, xo, yo, xr, yr, sr, xs, qv, acc, M, W, R, wp, wk, rk,
          ids, tab_v, tab_s, at_v, at_s, lsem, tsem, qsem, osem, xs_s, xs_r, ys_s, ys_r, sp_s, sp_r, id_s, id_r, *sums):
    y, x, c, z, s = where_am_i()
    gsum, csum = sums[:18], sums[18:]
    load_x = pltpu.make_async_copy(x_hbm, xin.at[pl.ds(0, 128)], lsem.at[0])
    load_y = pltpu.make_async_copy(y_hbm, yin.at[pl.ds(0, 128)], lsem.at[1])
    load_x.start()
    load_y.start()

    def space_at(k, j):
        a = ORDER[j]
        return space_of(y + a, x + a + lax.rem(k, 4), c + k // 4)

    barrier = pltpu.get_barrier_semaphore()
    for o in range(1, 32):
        pl.semaphore_signal(barrier, inc=1, device_id={"space": space_at(o // 4, o % 4)}, device_id_type=MESH)
    for d in (1, 2, 3):
        pl.semaphore_signal(barrier, inc=1, device_id={"snap": lax.rem(z + d, 4)}, device_id_type=MESH)

    xin[128] = jnp.zeros((128, 128), BF16)
    yin[128] = jnp.zeros((128, 128), BF16)
    slot, block = slot_tables(dest[...], y, x, c)
    tab_v[...] = jnp.broadcast_to(jnp.clip(slot, 0, 128), (8, 128))
    ids[s] = jnp.broadcast_to(block, (8, 128))
    tab_copy = pltpu.make_async_copy(tab_v, tab_s, tsem.at[0])
    tab_copy.start()
    tab_copy.wait()
    load_x.wait()

    def order_slots(src, dst, recv, k):
        def one(i):
            got = src[tab_s[0, i]]
            for q in range(4):
                dst[q, i] = got[32 * q:32 * q + 32]
            recv[z, i] = dst[z, i]

        loop(16 * k, 16 * k + 16, one)

    def over_z(src, recv, ss, rs, k):
        span = pl.ds(16 * k, 16)
        out = []
        for d in (1, 2, 3):
            to = lax.rem(z + d, 4)
            out.append(remote(src.at[to, span], recv.at[z, span], ss.at[k, d - 1], rs.at[k, d - 1], snap=to))
        return out

    def send_z(src, recv, ss, rs, k):
        for cp in over_z(src, recv, ss, rs, k):
            cp.start()

    order_slots(xin, xo, xr, 0)
    pl.semaphore_wait(barrier, 34)
    for k in range(1, CHUNKS):
        order_slots(xin, xo, xr, k)
        send_z(xo, xr, xs_s, xs_r, k - 1)
    load_y.wait()
    order_slots(yin, yo, yr, 0)
    send_z(xo, xr, xs_s, xs_r, CHUNKS - 1)

    def send_ids(k, j):
        o = 4 * k + j
        return remote(ids.at[s], ids.at[s], id_s.at[o], id_r.at[o], space=space_at(k, j))

    for o in range(1, 32):
        send_ids(o // 4, o % 4).start()
    loop(1, CHUNKS, lambda k: order_slots(yin, yo, yr, k))
    for k in range(FIRST_Y):
        send_z(yo, yr, ys_s, ys_r, k)

    for o in range(1, 32):
        send_ids(o // 4, o % 4).wait_recv()
    wanted = s * BLK_DEV + lax.broadcasted_iota(jnp.int32, (BLK_DEV, 1), 0)
    place = lax.rem(lax.broadcasted_iota(jnp.int32, (1, 128), 1), 4)
    found = jnp.zeros((BLK_DEV, 128), jnp.int32)
    for src in range(32):
        found = found + jnp.where(ids[src][0:1, :] == wanted, place + 4 * src, 0)
    found = jnp.sum(found, axis=1, keepdims=True)
    pick = lax.broadcasted_iota(jnp.int32, (BLK_DEV, 128), 0) == lax.broadcasted_iota(jnp.int32, (BLK_DEV, 128), 1)
    found = jnp.sum(jnp.where(pick, found, 0), axis=0, keepdims=True)
    at_v[...] = jnp.broadcast_to(jnp.clip(found, 0, 127), (8, 128))
    at_copy = pltpu.make_async_copy(at_v, at_s, tsem.at[1])
    at_copy.start()
    at_copy.wait()

    def to_slab(k, j):
        o = 4 * k + j
        return remote(xr.at[:, pl.ds(4 * o, 4)], sr.at[:, pl.ds(4 * s, 4)], sp_s.at[o], sp_r.at[o], space=space_at(k, j))

    def panel_rows(buf, k):
        return jnp.concatenate([buf[p, pl.ds(16 * k, 16)].reshape(512, 128) for p in range(4)], axis=1)

    acc[...] = jnp.zeros((512, 512), F32)
    contract = (((0,), (0,)), ((), ()))

    def forward(k):
        for j in range(4):
            to_slab(k, j).start()

    def gram_step(k):
        for cp in over_z(xo, xr, xs_s, xs_r, k):
            cp.wait_recv()

        @pl.when(k == 0)
        def _():
            sr[:, pl.ds(4 * s, 4)] = xr[:, 0:4]
            for j in range(1, 4):
                to_slab(0, j).start()

        @pl.when((k > 0) & (k < EARLY))
        def _():
            forward(k)

        rows = panel_rows(xr, k)
        acc[...] += lax.dot_general(rows, rows, contract, preferred_element_type=F32)

    loop(0, CHUNKS, gram_step)

    def later_y():
        for k in range(FIRST_Y, CHUNKS):
            send_z(yo, yr, ys_s, ys_r, k)

    b = 0
    for i in range(4):
        for j in range(i, 4):
            gsum[0][16 * b:16 * b + 16] = acc[128 * i:128 * i + 128, 128 * j:128 * j + 128].reshape(16, 8, 128)
            b += 1
    drain_g = all_sum(G_GROUPS, *gsum, after_z=later_y)
    loop(EARLY, CHUNKS, forward)
    full = gsum[7]
    b = 0
    for i in range(4):
        for j in range(i, 4):
            M[128 * i:128 * i + 128, 128 * j:128 * j + 128] = full[16 * b:16 * b + 16].reshape(128, 128) * (1.0 / ROWS)
            b += 1
    factor(M, R, W, wk, rk)
    out_r = pltpu.make_async_copy(R, r_out, osem.at[0])
    out_w = pltpu.make_async_copy(wp, w_out, osem.at[1])
    out_r.start()
    wp[0] = W[...].astype(BF16)
    wp[1] = (W[...] - wp[0].astype(F32)).astype(BF16)
    wp[2] = (W[...] - wp[0].astype(F32) - wp[1].astype(F32)).astype(BF16)
    out_w.start()

    last = (((1,), (1,)), ((), ()))

    def store_q(i):
        span = pl.ds(16 * i, 16)
        return pltpu.make_async_copy(qv.at[span], q_hbm.at[span], qsem.at[i])

    def form_basis():
        for o in range(1, 32):
            to_slab(o // 4, o % 4).wait_recv()

        def pick_block(i):
            at = at_s[0, i]
            for p in range(4):
                xs[i, :, 128 * p:128 * p + 128] = sr[p, at]

        loop(0, BLK_DEV, pick_block)
        def basis(i):
            span = pl.ds(16 * i, 16)
            rows = xs[span].reshape(512, 512)
            out = lax.dot_general(rows, wp[2], last, preferred_element_type=F32)
            out = out + lax.dot_general(rows, wp[1], last, preferred_element_type=F32)
            out = out + lax.dot_general(rows, wp[0], last, preferred_element_type=F32)
            qv[span] = out.reshape(16, 32, 512)
            store_q(i).start()

        loop(0, 4, basis)

    acc[...] = jnp.zeros((512, 512), F32)

    def cross_step(k):
        for cp in over_z(yo, yr, ys_s, ys_r, k):
            cp.wait_recv()
        acc[...] += lax.dot_general(panel_rows(xr, k), panel_rows(yr, k), contract, preferred_element_type=F32)

    loop(0, CHUNKS, cross_step)
    for j in range(4):
        csum[0][64 * j:64 * j + 64] = acc[:, 128 * j:128 * j + 128].reshape(64, 8, 128)
    drain_c = all_sum(C_GROUPS, *csum, after_scatter=form_basis)
    out_c = pltpu.make_async_copy(csum[7], c_out, osem.at[2])
    out_c.start()
    drain_g()
    drain_c()
    for o in range(1, 32):
        send_ids(o // 4, o % 4).wait_send()
        to_slab(o // 4, o % 4).wait_send()

    def drain_z(k):
        for cp in over_z(xo, xr, xs_s, xs_r, k) + over_z(yo, yr, ys_s, ys_r, k):
            cp.wait_send()

    loop(0, CHUNKS, drain_z)
    loop(0, 4, lambda i: store_q(i).wait())
    out_r.wait()
    out_w.wait()
    out_c.wait()


def finish(q_in, r_in, w_in, c_in, q_out, r_out, p_out, qv, R, W, C, cp, p, qi, qo, ii, oo):
    get_c = pltpu.make_async_copy(c_in, C, ii.at[0])
    get_w = pltpu.make_async_copy(w_in, W, ii.at[1])
    get_r = pltpu.make_async_copy(r_in, R, ii.at[2])
    parts = [pl.ds(16 * i, 16) for i in range(4)]
    gets = [pltpu.make_async_copy(q_in.at[t], qv.at[t], qi.at[i]) for i, t in enumerate(parts)]
    puts = [pltpu.make_async_copy(qv.at[t], q_out.at[t], qo.at[i]) for i, t in enumerate(parts)]
    put_r = pltpu.make_async_copy(R, r_out, oo.at[0])
    put_p = pltpu.make_async_copy(p, p_out, oo.at[1])
    get_c.start()
    get_w.start()
    for copy in gets:
        copy.start()
    get_r.start()
    get_c.wait()
    for j in range(4):
        rows = C[64 * j:64 * j + 64].reshape(512, 128)
        span = slice(128 * j, 128 * j + 128)
        c1 = rows.astype(BF16)
        c2 = (rows - c1.astype(F32)).astype(BF16)
        cp[0, :, span] = c1
        cp[1, :, span] = c2
        cp[2, :, span] = (rows - c1.astype(F32) - c2.astype(F32)).astype(BF16)
    get_w.wait()

    def term(i, j):
        return jnp.dot(W[i], cp[j], preferred_element_type=F32)

    for i in range(2):
        gets[i].wait()
        puts[i].start()
    p[...] = (term(2, 0) + term(0, 2) + term(1, 1) + term(1, 0) + term(0, 1) + term(0, 0)) * (1.0 / 512.0)
    put_p.start()
    for i in range(2, 4):
        gets[i].wait()
        puts[i].start()
    get_r.wait()
    put_r.start()
    for copy in puts:
        copy.wait()
    put_r.wait()
    put_p.wait()


def body(owned_x, owned_y, patch_dest):
    V = pl.BlockSpec(memory_space=pltpu.VMEM)
    A = pl.BlockSpec(memory_space=pl.ANY)
    dma = pltpu.SemaphoreType.DMA
    square = jax.ShapeDtypeStruct((512, 512), F32)
    panels = pltpu.VMEM((4, 128, 32, 128), BF16)
    basis, upper, inverse, cross = pl.pallas_call(
        whole,
        out_shape=(jax.ShapeDtypeStruct((BLK_DEV, 32, 512), F32), square, jax.ShapeDtypeStruct((3, 512, 512), BF16), jax.ShapeDtypeStruct((CT, 8, 128), F32)),
        in_specs=[V, A, A],
        out_specs=(A, A, A, A),
        scratch_shapes=[
            pltpu.VMEM((129, 128, 128), BF16),
            pltpu.VMEM((129, 128, 128), BF16),
            panels, panels, panels, panels, panels,
            pltpu.VMEM((BLK_DEV, 32, 512), BF16),
            pltpu.VMEM((BLK_DEV, 32, 512), F32),
            pltpu.VMEM((512, 512), F32),
            pltpu.VMEM((512, 512), F32),
            pltpu.VMEM((512, 512), F32),
            pltpu.VMEM((512, 512), F32),
            pltpu.VMEM((3, 512, 512), BF16),
            pltpu.VMEM((128, 128), F32),
            pltpu.VMEM((128, 128), F32),
            pltpu.VMEM((32, 8, 128), jnp.int32),
            pltpu.VMEM((8, 128), jnp.int32),
            pltpu.SMEM((8, 128), jnp.int32),
            pltpu.VMEM((8, 128), jnp.int32),
            pltpu.SMEM((8, 128), jnp.int32),
            dma((2,)), dma((2,)), dma((4,)), dma((3,)),
            dma((CHUNKS, 3)), dma((CHUNKS, 3)), dma((CHUNKS, 3)), dma((CHUNKS, 3)),
            dma((32,)), dma((32,)), dma((32,)), dma((32,)),
        ] + sum_scratch(G_GROUPS) + sum_scratch(C_GROUPS),
        compiler_params=pltpu.CompilerParams(
            collective_id=0, has_side_effects=True, vmem_limit_bytes=63 << 20
        ),
        name="window",
    )(patch_dest.reshape(1, 128), owned_x, owned_y)
    return pl.pallas_call(
        finish,
        out_shape=(jax.ShapeDtypeStruct((BLK_DEV, 32, 512), F32), square, square),
        in_specs=[A, A, A, A],
        out_specs=(A, A, A),
        scratch_shapes=[
            pltpu.VMEM((BLK_DEV, 32, 512), F32),
            pltpu.VMEM((512, 512), F32),
            pltpu.VMEM((3, 512, 512), BF16),
            pltpu.VMEM((CT, 8, 128), F32),
            pltpu.VMEM((3, 512, 512), BF16),
            pltpu.VMEM((512, 512), F32),
            dma((4,)), dma((4,)), dma((3,)), dma((2,)),
        ],
        compiler_params=pltpu.CompilerParams(vmem_limit_bytes=63 << 20),
        name="finish",
    )(basis, upper, inverse, cross)


def solution(mesh):
    in_specs = (P("space", None, "snap"), P("space", None, "snap"), P("space"))
    out_specs = (P("space", "snap", None), P(), P())
    return jax.shard_map(body, mesh=mesh, in_specs=in_specs, out_specs=out_specs, check_vma=False)
```

```python
import jax
import jax.numpy as jnp
from jax import lax
from jax.experimental import pallas as pl
from jax.experimental.pallas import tpu as pltpu
from jax.sharding import PartitionSpec as P

BLK_DEV = 64
HI = lax.Precision.HIGHEST

def small_inv(P, b):
    if b == 1:
        return [[1.0 / P[0][0]]]
    if b == 2:
        a, h, d = P[0][0], P[0][1], P[1][1]
        r = 1.0 / (a * d - h * h)
        return [[d * r, -h * r], [-h * r, a * r]]
    h = b // 2
    A = [[P[i][j] for j in range(h)] for i in range(h)]
    B = [[P[i][h + j] for j in range(h)] for i in range(h)]
    D = [[P[h + i][h + j] for j in range(h)] for i in range(h)]
    Ai = small_inv(A, h)
    AiB = [[sum(Ai[i][k] * B[k][j] for k in range(h)) for j in range(h)] for i in range(h)]
    S = [[None] * h for _ in range(h)]
    for i in range(h):
        for j in range(i, h):
            S[i][j] = D[i][j] - sum(B[k][i] * AiB[k][j] for k in range(h))
            S[j][i] = S[i][j]
    Si = small_inv(S, h)
    out = [[None] * b for _ in range(b)]
    BS = [[sum(AiB[i][k] * Si[k][j] for k in range(h)) for j in range(h)] for i in range(h)]
    for i in range(h):
        for j in range(h):
            out[h + i][h + j] = Si[i][j]
            out[i][h + j] = -BS[i][j]
            out[h + j][i] = -BS[i][j]
    for i in range(h):
        for j in range(i, h):
            v = Ai[i][j] + sum(BS[i][k] * AiB[j][k] for k in range(h))
            out[i][j] = v
            out[j][i] = v
    return out

def diag_block(D, b, r_out, w_out):
    lane = lax.broadcasted_iota(jnp.int32, (1, 128), 1)
    sub = lax.broadcasted_iota(jnp.int32, (8, 1), 0)
    M = list(D)
    for g in range(0, 128, b):
        v0, s0 = g // 8, g % 8
        r = [M[v0][s0 + s:s0 + s + 1, :] for s in range(b)]
        C0 = [jnp.broadcast_to(M[v0][:, g + t:g + t + 1], (8, 128)) for t in range(b)]
        P = [[C0[t][s0 + s:s0 + s + 1, :] for t in range(b)] for s in range(b)]
        ingroup = (lane >= g) & (lane < g + b)
        rp = [jnp.where(ingroup, jnp.where(lane == g + s, 1.0, 0.0), r[s]) for s in range(b)]
        if g + b < 128:
            Pi = small_inv(P, b)
            rt = [sum(Pi[s][t] * rp[t] for t in range(b)) for s in range(b)]
            for v in range(v0, 16):
                if v == v0 and s0 + b >= 8:
                    continue
                new = jnp.where(ingroup, 0.0, M[v])
                for s in range(b):
                    cs = C0[s] if v == v0 else M[v][:, g + s:g + s + 1]
                    new = new - cs * rt[s]
                if v == v0:
                    new = jnp.where(sub >= s0 + b, new, M[v])
                M[v] = new
        er, eb = list(r), list(rp)
        p = [list(row) for row in P]
        for s in range(b):
            sc = lax.rsqrt(p[s][s])
            for t in range(s + 1, b):
                m = p[s][t] / p[s][s]
                er[t] = er[t] - m * er[s]
                eb[t] = eb[t] - m * eb[s]
                for q in range(t, b):
                    p[t][q] = p[t][q] - m * p[s][q]
            r_out[g + s:g + s + 1, :] = jnp.where(lane >= g + s, er[s] * sc, 0.0)
            w_out[g + s:g + s + 1, :] = jnp.where(lane <= g + s, eb[s] * sc, 0.0)

def factor(M, R, W, wk, rk, nblk=4, b=4):
    n = nblk * 128
    colb = lax.broadcasted_iota(jnp.int32, (1, n), 1) // 128
    def outer(k, _):
        o = pl.multiple_of(k * 128, 128)
        kb = pl.ds(o, 128)
        D = [M[pl.ds(pl.multiple_of(o + 8 * v, 8), 8), kb] for v in range(16)]
        diag_block(D, b, rk, wk)
        M[kb, kb] = (lax.broadcasted_iota(jnp.int32, (128, 128), 0) == lax.broadcasted_iota(jnp.int32, (128, 128), 1)).astype(jnp.float32)
        row = jnp.dot(wk[...], M[kb, :], precision=HI, preferred_element_type=jnp.float32)
        M[kb, :] = row
        W[kb, :] = jnp.where(colb <= k, row, 0.0)
        R[kb, :] = jnp.where(colb > k, row, 0.0)
        R[kb, kb] = rk[...]
        def trail(i, _):
            ib = pl.ds(pl.multiple_of(i * 128, 128), 128)
            lik = M[kb, ib]
            upd = lax.dot_general(lik, M[kb, :], (((0,), (0,)), ((), ())), precision=HI, preferred_element_type=jnp.float32)
            M[ib, :] = jnp.where(colb == k, 0.0, M[ib, :]) - upd
            return 0
        lax.fori_loop(k + 1, nblk, trail, 0)
        return 0
    lax.fori_loop(0, nblk, outer, 0)


ROWS = 262144
MESH = pl.DeviceIdType.MESH
F32 = jnp.float32
BF16 = jnp.bfloat16
ORDER = (0, 2, 1, 3)
CHUNKS = 8
EARLY = 5
FIRST_Y = 2
CT = 256
G_GROUPS = ((0, 64), (64, 96))
C_GROUPS = ((0, 64), (64, 64), (128, 64), (192, 64))


def where_am_i():
    s = lax.axis_index("space")
    return s // 8, (s // 2) % 4, s % 2, lax.axis_index("snap"), s


def space_of(y, x, c):
    return (lax.rem(y, 4) * 4 + lax.rem(x, 4)) * 2 + lax.rem(c, 2)


def remote(src, dst, ss, rs, space=None, snap=None):
    dev = {}
    if space is not None:
        dev["space"] = space
    if snap is not None:
        dev["snap"] = snap
    return pltpu.make_async_remote_copy(
        src_ref=src, dst_ref=dst, send_sem=ss, recv_sem=rs, device_id=dev, device_id_type=MESH
    )


def loop(lo, hi, body):
    def step(i, carry):
        body(i)
        return carry

    lax.fori_loop(lo, hi, step, 0)


def await_bytes(ref, sem):
    pltpu.make_async_copy(ref, ref, sem).wait()


def column(row):
    eye = lax.broadcasted_iota(jnp.int32, (128, 128), 0) == lax.broadcasted_iota(jnp.int32, (128, 128), 1)
    return jnp.sum(jnp.where(eye, jnp.broadcast_to(row, (128, 128)), 0), axis=1, keepdims=True)


def slot_tables(dest, y, x, c):
    slab = jnp.where(dest >= 0, dest // BLK_DEV, -1)
    lane = lax.broadcasted_iota(jnp.int32, (128, 128), 1)
    sub = lax.broadcasted_iota(jnp.int32, (128, 128), 0)
    same = (column(slab) == slab) & (sub < lane)
    rank = jnp.sum(same.astype(jnp.int32), axis=0, keepdims=True)
    dy = (slab // 8 - y + 4) % 4
    dx = ((slab // 2) % 4 - x + 4) % 4
    dc = (slab % 2 - c + 2) % 2
    place = jnp.where(dy == 1, 2, jnp.where(dy == 2, 1, dy))
    pos = ((dc * 4 + (dx - dy + 4) % 4) * 4 + place) * 4 + rank
    pos = column(jnp.where(dest >= 0, pos, -1))
    hit = pos == lane
    slot = jnp.sum(jnp.where(hit, sub - 128, 0), axis=0, keepdims=True) + 128
    block = jnp.sum(jnp.where(hit, column(dest) + 1, 0), axis=0, keepdims=True) - 1
    return slot, block


def all_sum(groups, tiles, b1, half, b2, piece, zb, half2, full, ss, r1, r2, r3, r4, r5, after_scatter=None, after_z=None):
    y, x, c, z, s = where_am_i()
    chip = s // 2
    mate = chip * 2 + (1 - c)

    def chip_at(d):
        return lax.rem(y + d // 4, 4) * 4 + lax.rem(x + lax.rem(d, 4), 4)

    spans = [(g, at, n // 2, n // 32) for g, (at, n) in enumerate(groups)]

    def swap(g, at, h, m):
        return remote(tiles.at[pl.ds(at + (1 - c) * h, h)], b1.at[at // 2:at // 2 + h], ss.at[0], r1.at[g], space=mate)

    def scatter(g, at, h, m, d):
        q = chip_at(d)
        return remote(half.at[pl.ds(at // 2 + q * m, m)], b2.at[chip, at // 32:at // 32 + m], ss.at[1], r2.at[g], space=q * 2 + c)

    def across(g, at, h, m, d):
        mine = pl.ds(at // 32, m)
        return remote(piece.at[mine], zb.at[z, mine], ss.at[2], r3.at[g], snap=lax.rem(z + d, 4))

    def gather(g, at, h, m, d):
        mine = pl.ds(at // 2 + chip * m, m)
        return remote(half2.at[mine], half2.at[mine], ss.at[3], r4.at[g], space=chip_at(d) * 2 + c)

    def swap_back(g, at, h, m):
        return remote(half2.at[at // 2:at // 2 + h], full.at[pl.ds(at + c * h, h)], ss.at[4], r5.at[g], space=mate)

    for sp in spans:
        swap(*sp).start()
    for sp in spans:
        g, at, h, m = sp
        swap(*sp).wait_recv()
        half[at // 2:at // 2 + h] = tiles[pl.ds(at + c * h, h)] + b1[at // 2:at // 2 + h]
        loop(1, 16, lambda d: scatter(*sp, d).start())
        b2[chip, at // 32:at // 32 + m] = half[pl.ds(at // 2 + chip * m, m)]
    if after_scatter is not None:
        after_scatter()
    for sp in spans:
        g, at, h, m = sp
        mine = slice(at // 32, at // 32 + m)
        await_bytes(b2.at[0:15, mine], r2.at[g])
        total = b2[0, mine]
        for q in range(1, 16):
            total = total + b2[q, mine]
        piece[mine] = total
        for d in (1, 2, 3):
            across(*sp, d).start()
        zb[z, mine] = piece[mine]
    if after_z is not None:
        after_z()
    for sp in spans:
        g, at, h, m = sp
        mine = slice(at // 32, at // 32 + m)
        await_bytes(zb.at[0:3, mine], r3.at[g])
        half2[pl.ds(at // 2 + chip * m, m)] = zb[0, mine] + zb[1, mine] + zb[2, mine] + zb[3, mine]
        loop(1, 16, lambda d: gather(*sp, d).start())
    for sp in spans:
        g, at, h, m = sp
        await_bytes(b2.at[0:15, at // 32:at // 32 + m], r4.at[g])
        swap_back(*sp).start()
        full[pl.ds(at + c * h, h)] = half2[at // 2:at // 2 + h]
    for sp in spans:
        swap_back(*sp).wait_recv()

    def drain():
        for stage, sent in enumerate((b1, b2.at[0:15], zb.at[0:3], b2.at[0:15], b1)):
            await_bytes(sent, ss.at[stage])

    return drain


def sum_scratch(groups):
    n = sum(size for _, size in groups)
    k = len(groups)
    h, m = n // 2, n // 32
    dma = pltpu.SemaphoreType.DMA
    return [
        pltpu.VMEM((n, 8, 128), F32),
        pltpu.VMEM((h, 8, 128), F32),
        pltpu.VMEM((h, 8, 128), F32),
        pltpu.VMEM((16, m, 8, 128), F32),
        pltpu.VMEM((m, 8, 128), F32),
        pltpu.VMEM((4, m, 8, 128), F32),
        pltpu.VMEM((h, 8, 128), F32),
        pltpu.VMEM((n, 8, 128), F32),
        dma((5,)), dma((k,)), dma((k,)), dma((k,)), dma((k,)), dma((k,)),
    ]


def whole(dest, x_hbm, y_hbm, q_hbm, r_out, w_out, c_out, xin, yin, xo, yo, xr, yr, sr, xs, qv, acc, M, W, R, wp, wk, rk,
          ids, tab_v, tab_s, at_v, at_s, lsem, tsem, qsem, osem, xs_s, xs_r, ys_s, ys_r, sp_s, sp_r, id_s, id_r, *sums):
    y, x, c, z, s = where_am_i()
    gsum, csum = sums[:14], sums[14:]
    load_x = pltpu.make_async_copy(x_hbm, xin.at[pl.ds(0, 128)], lsem.at[0])
    load_y = pltpu.make_async_copy(y_hbm, yin.at[pl.ds(0, 128)], lsem.at[1])
    load_x.start()
    load_y.start()

    def space_at(k, j):
        a = ORDER[j]
        return space_of(y + a, x + a + lax.rem(k, 4), c + k // 4)

    barrier = pltpu.get_barrier_semaphore()
    for o in range(1, 32):
        pl.semaphore_signal(barrier, inc=1, device_id={"space": space_at(o // 4, o % 4)}, device_id_type=MESH)
    for d in (1, 2, 3):
        pl.semaphore_signal(barrier, inc=1, device_id={"snap": lax.rem(z + d, 4)}, device_id_type=MESH)

    xin[128] = jnp.zeros((128, 128), BF16)
    yin[128] = jnp.zeros((128, 128), BF16)
    slot, block = slot_tables(dest[...], y, x, c)
    tab_v[...] = jnp.broadcast_to(jnp.clip(slot, 0, 128), (8, 128))
    ids[s] = jnp.broadcast_to(block, (8, 128))
    tab_copy = pltpu.make_async_copy(tab_v, tab_s, tsem.at[0])
    tab_copy.start()
    tab_copy.wait()
    load_x.wait()

    def order_slots(src, dst, recv, k):
        def one(i):
            got = src[tab_s[0, i]]
            for q in range(4):
                dst[q, i] = got[32 * q:32 * q + 32]
            recv[z, i] = dst[z, i]

        loop(16 * k, 16 * k + 16, one)

    def over_z(src, recv, ss, rs, k):
        span = pl.ds(16 * k, 16)
        out = []
        for d in (1, 2, 3):
            to = lax.rem(z + d, 4)
            out.append(remote(src.at[to, span], recv.at[z, span], ss.at[0], rs.at[k], snap=to))
        return out

    def send_z(src, recv, ss, rs, k):
        for cp in over_z(src, recv, ss, rs, k):
            cp.start()

    order_slots(xin, xo, xr, 0)
    pl.semaphore_wait(barrier, 34)
    for k in range(1, CHUNKS):
        order_slots(xin, xo, xr, k)
        send_z(xo, xr, xs_s, xs_r, k - 1)
    load_y.wait()
    order_slots(yin, yo, yr, 0)
    send_z(xo, xr, xs_s, xs_r, CHUNKS - 1)

    def send_ids(k, j):
        return remote(ids.at[s], ids.at[s], id_s.at[0], id_r.at[0], space=space_at(k, j))

    for o in range(1, 32):
        send_ids(o // 4, o % 4).start()
    loop(1, CHUNKS, lambda k: order_slots(yin, yo, yr, k))
    for k in range(FIRST_Y):
        send_z(yo, yr, ys_s, ys_r, k)

    await_bytes(ids.at[0:31], id_r.at[0])
    wanted = s * BLK_DEV + lax.broadcasted_iota(jnp.int32, (BLK_DEV, 1), 0)
    place = lax.rem(lax.broadcasted_iota(jnp.int32, (1, 128), 1), 4)
    found = jnp.zeros((BLK_DEV, 128), jnp.int32)
    for src in range(32):
        found = found + jnp.where(ids[src][0:1, :] == wanted, place + 4 * src, 0)
    found = jnp.sum(found, axis=1, keepdims=True)
    pick = lax.broadcasted_iota(jnp.int32, (BLK_DEV, 128), 0) == lax.broadcasted_iota(jnp.int32, (BLK_DEV, 128), 1)
    found = jnp.sum(jnp.where(pick, found, 0), axis=0, keepdims=True)
    at_v[...] = jnp.broadcast_to(jnp.clip(found, 0, 127), (8, 128))
    at_copy = pltpu.make_async_copy(at_v, at_s, tsem.at[1])
    at_copy.start()
    at_copy.wait()

    def to_slab(k, j):
        o = 4 * k + j
        return remote(xr.at[:, pl.ds(4 * o, 4)], sr.at[:, pl.ds(4 * s, 4)], sp_s.at[0], sp_r.at[0], space=space_at(k, j))

    def panel_rows(buf, k):
        return jnp.concatenate([buf[p, pl.ds(16 * k, 16)].reshape(512, 128) for p in range(4)], axis=1)

    acc[...] = jnp.zeros((512, 512), F32)
    contract = (((0,), (0,)), ((), ()))

    def forward(k):
        for j in range(4):
            to_slab(k, j).start()

    def gram_step(k):
        await_bytes(xr.at[0:3, pl.ds(16 * k, 16)], xs_r.at[k])

        @pl.when(k == 0)
        def _():
            sr[:, pl.ds(4 * s, 4)] = xr[:, 0:4]
            for j in range(1, 4):
                to_slab(0, j).start()

        @pl.when((k > 0) & (k < EARLY))
        def _():
            forward(k)

        rows = panel_rows(xr, k)
        acc[...] += lax.dot_general(rows, rows, contract, preferred_element_type=F32)

    loop(0, CHUNKS, gram_step)

    def later_y():
        for k in range(FIRST_Y, CHUNKS):
            send_z(yo, yr, ys_s, ys_r, k)

    b = 0
    for i in range(4):
        for j in range(i, 4):
            gsum[0][16 * b:16 * b + 16] = acc[128 * i:128 * i + 128, 128 * j:128 * j + 128].reshape(16, 8, 128)
            b += 1
    drain_g = all_sum(G_GROUPS, *gsum, after_z=later_y)
    loop(EARLY, CHUNKS, forward)
    full = gsum[7]
    b = 0
    for i in range(4):
        for j in range(i, 4):
            M[128 * i:128 * i + 128, 128 * j:128 * j + 128] = full[16 * b:16 * b + 16].reshape(128, 128) * (1.0 / ROWS)
            b += 1
    factor(M, R, W, wk, rk)
    out_r = pltpu.make_async_copy(R, r_out, osem.at[0])
    out_w = pltpu.make_async_copy(wp, w_out, osem.at[1])
    out_r.start()
    wp[0] = W[...].astype(BF16)
    wp[1] = (W[...] - wp[0].astype(F32)).astype(BF16)
    wp[2] = (W[...] - wp[0].astype(F32) - wp[1].astype(F32)).astype(BF16)
    out_w.start()

    last = (((1,), (1,)), ((), ()))

    def store_q(i):
        span = pl.ds(16 * i, 16)
        return pltpu.make_async_copy(qv.at[span], q_hbm.at[span], qsem.at[i])

    def form_basis():
        await_bytes(sr.at[:, 0:124], sp_r.at[0])

        def pick_block(i):
            at = at_s[0, i]
            for p in range(4):
                xs[i, :, 128 * p:128 * p + 128] = sr[p, at]

        loop(0, BLK_DEV, pick_block)
        def basis(i):
            span = pl.ds(16 * i, 16)
            rows = xs[span].reshape(512, 512)
            out = lax.dot_general(rows, wp[2], last, preferred_element_type=F32)
            out = out + lax.dot_general(rows, wp[1], last, preferred_element_type=F32)
            out = out + lax.dot_general(rows, wp[0], last, preferred_element_type=F32)
            qv[span] = out.reshape(16, 32, 512)
            store_q(i).start()

        loop(0, 4, basis)

    acc[...] = jnp.zeros((512, 512), F32)

    def cross_step(k):
        await_bytes(yr.at[0:3, pl.ds(16 * k, 16)], ys_r.at[k])
        acc[...] += lax.dot_general(panel_rows(xr, k), panel_rows(yr, k), contract, preferred_element_type=F32)

    loop(0, CHUNKS, cross_step)
    for j in range(4):
        csum[0][64 * j:64 * j + 64] = acc[:, 128 * j:128 * j + 128].reshape(64, 8, 128)
    drain_c = all_sum(C_GROUPS, *csum, after_scatter=form_basis)
    out_c = pltpu.make_async_copy(csum[7], c_out, osem.at[2])
    out_c.start()
    drain_g()
    drain_c()
    await_bytes(ids.at[0:31], id_s.at[0])
    await_bytes(sr.at[:, 0:124], sp_s.at[0])
    await_bytes(xo.at[0:3], xs_s.at[0])
    await_bytes(yo.at[0:3], ys_s.at[0])
    loop(0, 4, lambda i: store_q(i).wait())
    out_r.wait()
    out_w.wait()
    out_c.wait()


def finish(q_in, r_in, w_in, c_in, q_out, r_out, p_out, qv, R, W, C, cp, p, qi, qo, ii, oo):
    get_c = pltpu.make_async_copy(c_in, C, ii.at[0])
    get_w = pltpu.make_async_copy(w_in, W, ii.at[1])
    get_r = pltpu.make_async_copy(r_in, R, ii.at[2])
    parts = [pl.ds(16 * i, 16) for i in range(4)]
    gets = [pltpu.make_async_copy(q_in.at[t], qv.at[t], qi.at[i]) for i, t in enumerate(parts)]
    puts = [pltpu.make_async_copy(qv.at[t], q_out.at[t], qo.at[i]) for i, t in enumerate(parts)]
    put_r = pltpu.make_async_copy(R, r_out, oo.at[0])
    put_p = pltpu.make_async_copy(p, p_out, oo.at[1])
    get_c.start()
    get_w.start()
    for copy in gets:
        copy.start()
    get_r.start()
    get_c.wait()
    for j in range(4):
        rows = C[64 * j:64 * j + 64].reshape(512, 128)
        span = slice(128 * j, 128 * j + 128)
        c1 = rows.astype(BF16)
        c2 = (rows - c1.astype(F32)).astype(BF16)
        cp[0, :, span] = c1
        cp[1, :, span] = c2
        cp[2, :, span] = (rows - c1.astype(F32) - c2.astype(F32)).astype(BF16)
    get_w.wait()

    def term(i, j):
        return jnp.dot(W[i], cp[j], preferred_element_type=F32)

    for i in range(2):
        gets[i].wait()
        puts[i].start()
    p[...] = (term(2, 0) + term(0, 2) + term(1, 1) + term(1, 0) + term(0, 1) + term(0, 0)) * (1.0 / 512.0)
    put_p.start()
    for i in range(2, 4):
        gets[i].wait()
        puts[i].start()
    get_r.wait()
    put_r.start()
    for copy in puts:
        copy.wait()
    put_r.wait()
    put_p.wait()


def body(owned_x, owned_y, patch_dest):
    V = pl.BlockSpec(memory_space=pltpu.VMEM)
    A = pl.BlockSpec(memory_space=pl.ANY)
    dma = pltpu.SemaphoreType.DMA
    square = jax.ShapeDtypeStruct((512, 512), F32)
    panels = pltpu.VMEM((4, 128, 32, 128), BF16)
    basis, upper, inverse, cross = pl.pallas_call(
        whole,
        out_shape=(jax.ShapeDtypeStruct((BLK_DEV, 32, 512), F32), square, jax.ShapeDtypeStruct((3, 512, 512), BF16), jax.ShapeDtypeStruct((CT, 8, 128), F32)),
        in_specs=[V, A, A],
        out_specs=(A, A, A, A),
        scratch_shapes=[
            pltpu.VMEM((129, 128, 128), BF16),
            pltpu.VMEM((129, 128, 128), BF16),
            panels, panels, panels, panels, panels,
            pltpu.VMEM((BLK_DEV, 32, 512), BF16),
            pltpu.VMEM((BLK_DEV, 32, 512), F32),
            pltpu.VMEM((512, 512), F32),
            pltpu.VMEM((512, 512), F32),
            pltpu.VMEM((512, 512), F32),
            pltpu.VMEM((512, 512), F32),
            pltpu.VMEM((3, 512, 512), BF16),
            pltpu.VMEM((128, 128), F32),
            pltpu.VMEM((128, 128), F32),
            pltpu.VMEM((32, 8, 128), jnp.int32),
            pltpu.VMEM((8, 128), jnp.int32),
            pltpu.SMEM((8, 128), jnp.int32),
            pltpu.VMEM((8, 128), jnp.int32),
            pltpu.SMEM((8, 128), jnp.int32),
            dma((2,)), dma((2,)), dma((4,)), dma((3,)),
            dma((1,)), dma((CHUNKS,)), dma((1,)), dma((CHUNKS,)),
            dma((1,)), dma((1,)), dma((1,)), dma((1,)),
        ] + sum_scratch(G_GROUPS) + sum_scratch(C_GROUPS),
        compiler_params=pltpu.CompilerParams(
            collective_id=0, has_side_effects=True, vmem_limit_bytes=63 << 20
        ),
        name="window",
    )(patch_dest.reshape(1, 128), owned_x, owned_y)
    return pl.pallas_call(
        finish,
        out_shape=(jax.ShapeDtypeStruct((BLK_DEV, 32, 512), F32), square, square),
        in_specs=[A, A, A, A],
        out_specs=(A, A, A),
        scratch_shapes=[
            pltpu.VMEM((BLK_DEV, 32, 512), F32),
            pltpu.VMEM((512, 512), F32),
            pltpu.VMEM((3, 512, 512), BF16),
            pltpu.VMEM((CT, 8, 128), F32),
            pltpu.VMEM((3, 512, 512), BF16),
            pltpu.VMEM((512, 512), F32),
            dma((4,)), dma((4,)), dma((3,)), dma((2,)),
        ],
        compiler_params=pltpu.CompilerParams(vmem_limit_bytes=63 << 20),
        name="finish",
    )(basis, upper, inverse, cross)


def solution(mesh):
    in_specs = (P("space", None, "snap"), P("space", None, "snap"), P("space"))
    out_specs = (P("space", "snap", None), P(), P())
    return jax.shard_map(body, mesh=mesh, in_specs=in_specs, out_specs=out_specs, check_vma=False)
```

```python
import jax
import jax.numpy as jnp
from jax import lax
from jax.experimental import pallas as pl
from jax.experimental.pallas import tpu as pltpu
from jax.sharding import PartitionSpec as P

BLK_DEV = 64
HI = lax.Precision.HIGHEST

def small_inv(P, b):
    if b == 1:
        return [[1.0 / P[0][0]]]
    if b == 2:
        a, h, d = P[0][0], P[0][1], P[1][1]
        r = 1.0 / (a * d - h * h)
        return [[d * r, -h * r], [-h * r, a * r]]
    h = b // 2
    A = [[P[i][j] for j in range(h)] for i in range(h)]
    B = [[P[i][h + j] for j in range(h)] for i in range(h)]
    D = [[P[h + i][h + j] for j in range(h)] for i in range(h)]
    Ai = small_inv(A, h)
    AiB = [[sum(Ai[i][k] * B[k][j] for k in range(h)) for j in range(h)] for i in range(h)]
    S = [[None] * h for _ in range(h)]
    for i in range(h):
        for j in range(i, h):
            S[i][j] = D[i][j] - sum(B[k][i] * AiB[k][j] for k in range(h))
            S[j][i] = S[i][j]
    Si = small_inv(S, h)
    out = [[None] * b for _ in range(b)]
    BS = [[sum(AiB[i][k] * Si[k][j] for k in range(h)) for j in range(h)] for i in range(h)]
    for i in range(h):
        for j in range(h):
            out[h + i][h + j] = Si[i][j]
            out[i][h + j] = -BS[i][j]
            out[h + j][i] = -BS[i][j]
    for i in range(h):
        for j in range(i, h):
            v = Ai[i][j] + sum(BS[i][k] * AiB[j][k] for k in range(h))
            out[i][j] = v
            out[j][i] = v
    return out

def diag_block(D, b, r_out, w_out):
    lane = lax.broadcasted_iota(jnp.int32, (1, 128), 1)
    sub = lax.broadcasted_iota(jnp.int32, (8, 1), 0)
    M = list(D)
    for g in range(0, 128, b):
        v0, s0 = g // 8, g % 8
        r = [M[v0][s0 + s:s0 + s + 1, :] for s in range(b)]
        C0 = [jnp.broadcast_to(M[v0][:, g + t:g + t + 1], (8, 128)) for t in range(b)]
        P = [[C0[t][s0 + s:s0 + s + 1, :] for t in range(b)] for s in range(b)]
        ingroup = (lane >= g) & (lane < g + b)
        rp = [jnp.where(ingroup, jnp.where(lane == g + s, 1.0, 0.0), r[s]) for s in range(b)]
        if g + b < 128:
            Pi = small_inv(P, b)
            rt = [sum(Pi[s][t] * rp[t] for t in range(b)) for s in range(b)]
            for v in range(v0, 16):
                if v == v0 and s0 + b >= 8:
                    continue
                new = jnp.where(ingroup, 0.0, M[v])
                for s in range(b):
                    cs = C0[s] if v == v0 else M[v][:, g + s:g + s + 1]
                    new = new - cs * rt[s]
                if v == v0:
                    new = jnp.where(sub >= s0 + b, new, M[v])
                M[v] = new
        er, eb = list(r), list(rp)
        p = [list(row) for row in P]
        for s in range(b):
            sc = lax.rsqrt(p[s][s])
            for t in range(s + 1, b):
                m = p[s][t] / p[s][s]
                er[t] = er[t] - m * er[s]
                eb[t] = eb[t] - m * eb[s]
                for q in range(t, b):
                    p[t][q] = p[t][q] - m * p[s][q]
            r_out[g + s:g + s + 1, :] = jnp.where(lane >= g + s, er[s] * sc, 0.0)
            w_out[g + s:g + s + 1, :] = jnp.where(lane <= g + s, eb[s] * sc, 0.0)

def factor(M, R, W, wk, rk, nblk=4, b=4):
    n = nblk * 128
    colb = lax.broadcasted_iota(jnp.int32, (1, n), 1) // 128
    def outer(k, _):
        o = pl.multiple_of(k * 128, 128)
        kb = pl.ds(o, 128)
        D = [M[pl.ds(pl.multiple_of(o + 8 * v, 8), 8), kb] for v in range(16)]
        diag_block(D, b, rk, wk)
        M[kb, kb] = (lax.broadcasted_iota(jnp.int32, (128, 128), 0) == lax.broadcasted_iota(jnp.int32, (128, 128), 1)).astype(jnp.float32)
        row = jnp.dot(wk[...], M[kb, :], precision=HI, preferred_element_type=jnp.float32)
        M[kb, :] = row
        W[kb, :] = jnp.where(colb <= k, row, 0.0)
        R[kb, :] = jnp.where(colb > k, row, 0.0)
        R[kb, kb] = rk[...]
        def trail(i, _):
            ib = pl.ds(pl.multiple_of(i * 128, 128), 128)
            lik = M[kb, ib]
            upd = lax.dot_general(lik, M[kb, :], (((0,), (0,)), ((), ())), precision=HI, preferred_element_type=jnp.float32)
            M[ib, :] = jnp.where(colb == k, 0.0, M[ib, :]) - upd
            return 0
        lax.fori_loop(k + 1, nblk, trail, 0)
        return 0
    lax.fori_loop(0, nblk, outer, 0)


ROWS = 262144
MESH = pl.DeviceIdType.MESH
F32 = jnp.float32
BF16 = jnp.bfloat16
ORDER = (0, 2, 1, 3)
CHUNKS = 8
EARLY = 5
FIRST_Y = 2
CT = 256
G_GROUPS = ((0, 64), (64, 96))
C_GROUPS = ((0, 64), (64, 64), (128, 64), (192, 64))


def where_am_i():
    s = lax.axis_index("space")
    return s // 8, (s // 2) % 4, s % 2, lax.axis_index("snap"), s


def space_of(y, x, c):
    return (lax.rem(y, 4) * 4 + lax.rem(x, 4)) * 2 + lax.rem(c, 2)


def remote(src, dst, ss, rs, space=None, snap=None):
    dev = {}
    if space is not None:
        dev["space"] = space
    if snap is not None:
        dev["snap"] = snap
    return pltpu.make_async_remote_copy(
        src_ref=src, dst_ref=dst, send_sem=ss, recv_sem=rs, device_id=dev, device_id_type=MESH
    )


def loop(lo, hi, body):
    def step(i, carry):
        body(i)
        return carry

    lax.fori_loop(lo, hi, step, 0)


def await_bytes(ref, sem):
    pltpu.make_async_copy(ref, ref, sem).wait()


def column(row):
    eye = lax.broadcasted_iota(jnp.int32, (128, 128), 0) == lax.broadcasted_iota(jnp.int32, (128, 128), 1)
    return jnp.sum(jnp.where(eye, jnp.broadcast_to(row, (128, 128)), 0), axis=1, keepdims=True)


def slot_tables(dest, y, x, c):
    slab = jnp.where(dest >= 0, dest // BLK_DEV, -1)
    lane = lax.broadcasted_iota(jnp.int32, (128, 128), 1)
    sub = lax.broadcasted_iota(jnp.int32, (128, 128), 0)
    same = (column(slab) == slab) & (sub < lane)
    rank = jnp.sum(same.astype(jnp.int32), axis=0, keepdims=True)
    dy = (slab // 8 - y + 4) % 4
    dx = ((slab // 2) % 4 - x + 4) % 4
    dc = (slab % 2 - c + 2) % 2
    place = jnp.where(dy == 1, 2, jnp.where(dy == 2, 1, dy))
    pos = ((dc * 4 + (dx - dy + 4) % 4) * 4 + place) * 4 + rank
    pos = column(jnp.where(dest >= 0, pos, -1))
    hit = pos == lane
    slot = jnp.sum(jnp.where(hit, sub - 128, 0), axis=0, keepdims=True) + 128
    block = jnp.sum(jnp.where(hit, column(dest) + 1, 0), axis=0, keepdims=True) - 1
    return slot, block


def all_sum(groups, tiles, b1, half, b2, piece, zb, half2, full, ss, r1, r2, r3, r4, r5, keep, after_scatter=None, after_z=None):
    y, x, c, z, s = where_am_i()
    chip = s // 2
    mate = chip * 2 + (1 - c)

    def chip_at(d):
        return lax.rem(y + d // 4, 4) * 4 + lax.rem(x + lax.rem(d, 4), 4)

    spans = [(g, at, n // 2, n // 32) for g, (at, n) in enumerate(groups)]

    def swap(g, at, h, m):
        return remote(tiles.at[pl.ds(at + (1 - c) * h, h)], b1.at[at // 2:at // 2 + h], ss.at[0], r1.at[g], space=mate)

    def scatter(g, at, h, m, d):
        q = chip_at(d)
        return remote(half.at[pl.ds(at // 2 + q * m, m)], b2.at[chip, at // 32:at // 32 + m], ss.at[1], r2.at[g], space=q * 2 + c)

    def across(g, at, h, m, d):
        mine = pl.ds(at // 32, m)
        return remote(piece.at[mine], zb.at[z, mine], ss.at[2], r3.at[g], snap=lax.rem(z + d, 4))

    def gather(g, at, h, m, d):
        mine = pl.ds(at // 2 + chip * m, m)
        return remote(half2.at[mine], half2.at[mine], ss.at[3], r4.at[g], space=chip_at(d) * 2 + c)

    def swap_back(g, at, h, m):
        return remote(half2.at[at // 2:at // 2 + h], full.at[pl.ds(at + c * h, h)], ss.at[4], r5.at[g], space=mate)

    for sp in spans:
        swap(*sp).start()
    for sp in spans:
        g, at, h, m = sp
        swap(*sp).wait_recv()
        half[at // 2:at // 2 + h] = tiles[pl.ds(at + c * h, h)] + b1[at // 2:at // 2 + h]
        loop(1, 16, lambda d: scatter(*sp, d).start())
        b2[chip, at // 32:at // 32 + m] = half[pl.ds(at // 2 + chip * m, m)]
    if after_scatter is not None:
        after_scatter()
    for sp in spans:
        g, at, h, m = sp
        mine = slice(at // 32, at // 32 + m)
        await_bytes(b2.at[0:15, mine], r2.at[g])
        total = b2[0, mine]
        for q in range(1, 16):
            total = total + b2[q, mine]
        piece[mine] = total
        for d in (1, 2, 3):
            across(*sp, d).start()
        zb[z, mine] = piece[mine]
    if after_z is not None:
        after_z()
    for sp in spans:
        g, at, h, m = sp
        mine = slice(at // 32, at // 32 + m)
        await_bytes(zb.at[0:3, mine], r3.at[g])
        half2[pl.ds(at // 2 + chip * m, m)] = zb[0, mine] + zb[1, mine] + zb[2, mine] + zb[3, mine]
        loop(1, 16, lambda d: gather(*sp, d).start())
    for sp in spans:
        g, at, h, m = sp
        await_bytes(b2.at[0:15, at // 32:at // 32 + m], r4.at[g])
        swap_back(*sp).start()
        keep(half2.at[at // 2:at // 2 + h], full.at[pl.ds(at + c * h, h)])
    for sp in spans:
        swap_back(*sp).wait_recv()

    def drain():
        for stage, sent in enumerate((b1, b2.at[0:15], zb.at[0:3], b2.at[0:15], b1)):
            await_bytes(sent, ss.at[stage])

    return drain


def sum_scratch(groups, with_full):
    n = sum(size for _, size in groups)
    k = len(groups)
    h, m = n // 2, n // 32
    dma = pltpu.SemaphoreType.DMA
    return [
        pltpu.VMEM((n, 8, 128), F32),
        pltpu.VMEM((h, 8, 128), F32),
        pltpu.VMEM((h, 8, 128), F32),
        pltpu.VMEM((16, m, 8, 128), F32),
        pltpu.VMEM((m, 8, 128), F32),
        pltpu.VMEM((4, m, 8, 128), F32),
        pltpu.VMEM((h, 8, 128), F32),
    ] + [pltpu.VMEM((n, 8, 128), F32)] * with_full + [dma((5,))] + [dma((k,))] * 5


def whole(dest, x_hbm, y_hbm, q_hbm, r_out, w_out, c_out, xin, yin, xo, yo, xr, yr, sr, xs, qv, acc, M, W, R, wp, wk, rk,
          ids, tab_v, tab_s, at_v, at_s, lsem, tsem, qsem, osem, xs_s, xs_r, ys_s, ys_r, sp_s, sp_r, id_s, id_r, *sums):
    y, x, c, z, s = where_am_i()
    gsum, csum = sums[:14], sums[14:]
    load_x = pltpu.make_async_copy(x_hbm, xin.at[pl.ds(0, 128)], lsem.at[0])
    load_y = pltpu.make_async_copy(y_hbm, yin.at[pl.ds(0, 128)], lsem.at[1])
    load_x.start()
    load_y.start()

    def space_at(k, j):
        a = ORDER[j]
        return space_of(y + a, x + a + lax.rem(k, 4), c + k // 4)

    barrier = pltpu.get_barrier_semaphore()
    for o in range(1, 32):
        pl.semaphore_signal(barrier, inc=1, device_id={"space": space_at(o // 4, o % 4)}, device_id_type=MESH)
    for d in (1, 2, 3):
        pl.semaphore_signal(barrier, inc=1, device_id={"snap": lax.rem(z + d, 4)}, device_id_type=MESH)

    xin[128] = jnp.zeros((128, 128), BF16)
    yin[128] = jnp.zeros((128, 128), BF16)
    slot, block = slot_tables(dest[...], y, x, c)
    tab_v[...] = jnp.broadcast_to(jnp.clip(slot, 0, 128), (8, 128))
    ids[s] = jnp.broadcast_to(block, (8, 128))
    tab_copy = pltpu.make_async_copy(tab_v, tab_s, tsem.at[0])
    tab_copy.start()
    tab_copy.wait()
    load_x.wait()

    def order_slots(src, dst, recv, k):
        def one(i):
            got = src[tab_s[0, i]]
            for q in range(4):
                dst[q, i] = got[32 * q:32 * q + 32]
            recv[z, i] = dst[z, i]

        loop(16 * k, 16 * k + 16, one)

    def over_z(src, recv, ss, rs, k):
        span = pl.ds(16 * k, 16)
        out = []
        for d in (1, 2, 3):
            to = lax.rem(z + d, 4)
            out.append(remote(src.at[to, span], recv.at[z, span], ss.at[0], rs.at[k], snap=to))
        return out

    def send_z(src, recv, ss, rs, k):
        for cp in over_z(src, recv, ss, rs, k):
            cp.start()

    order_slots(xin, xo, xr, 0)
    pl.semaphore_wait(barrier, 34)
    for k in range(1, CHUNKS):
        order_slots(xin, xo, xr, k)
        send_z(xo, xr, xs_s, xs_r, k - 1)
    load_y.wait()
    order_slots(yin, yo, yr, 0)
    send_z(xo, xr, xs_s, xs_r, CHUNKS - 1)

    def send_ids(k, j):
        return remote(ids.at[s], ids.at[s], id_s.at[0], id_r.at[0], space=space_at(k, j))

    for o in range(1, 32):
        send_ids(o // 4, o % 4).start()
    loop(1, CHUNKS, lambda k: order_slots(yin, yo, yr, k))
    for k in range(FIRST_Y):
        send_z(yo, yr, ys_s, ys_r, k)

    await_bytes(ids.at[0:31], id_r.at[0])
    wanted = s * BLK_DEV + lax.broadcasted_iota(jnp.int32, (BLK_DEV, 1), 0)
    place = lax.rem(lax.broadcasted_iota(jnp.int32, (1, 128), 1), 4)
    found = jnp.zeros((BLK_DEV, 128), jnp.int32)
    for src in range(32):
        found = found + jnp.where(ids[src][0:1, :] == wanted, place + 4 * src, 0)
    found = jnp.sum(found, axis=1, keepdims=True)
    pick = lax.broadcasted_iota(jnp.int32, (BLK_DEV, 128), 0) == lax.broadcasted_iota(jnp.int32, (BLK_DEV, 128), 1)
    found = jnp.sum(jnp.where(pick, found, 0), axis=0, keepdims=True)
    at_v[...] = jnp.broadcast_to(jnp.clip(found, 0, 127), (8, 128))
    at_copy = pltpu.make_async_copy(at_v, at_s, tsem.at[1])
    at_copy.start()
    at_copy.wait()

    def to_slab(k, j):
        o = 4 * k + j
        return remote(xr.at[:, pl.ds(4 * o, 4)], sr.at[:, pl.ds(4 * s, 4)], sp_s.at[0], sp_r.at[0], space=space_at(k, j))

    def panel_rows(buf, k):
        return jnp.concatenate([buf[p, pl.ds(16 * k, 16)].reshape(512, 128) for p in range(4)], axis=1)

    acc[...] = jnp.zeros((512, 512), F32)
    contract = (((0,), (0,)), ((), ()))

    def forward(k):
        for j in range(4):
            to_slab(k, j).start()

    def gram_step(k):
        await_bytes(xr.at[0:3, pl.ds(16 * k, 16)], xs_r.at[k])

        @pl.when(k == 0)
        def _():
            sr[:, pl.ds(4 * s, 4)] = xr[:, 0:4]
            for j in range(1, 4):
                to_slab(0, j).start()

        @pl.when((k > 0) & (k < EARLY))
        def _():
            forward(k)

        rows = panel_rows(xr, k)
        acc[...] += lax.dot_general(rows, rows, contract, preferred_element_type=F32)

    loop(0, CHUNKS, gram_step)

    def later_y():
        for k in range(FIRST_Y, CHUNKS):
            send_z(yo, yr, ys_s, ys_r, k)

    b = 0
    for i in range(4):
        for j in range(i, 4):
            gsum[0][16 * b:16 * b + 16] = acc[128 * i:128 * i + 128, 128 * j:128 * j + 128].reshape(16, 8, 128)
            b += 1
    def store_half(src, dst):
        dst[...] = src[...]

    drain_g = all_sum(G_GROUPS, *gsum, keep=store_half, after_z=later_y)
    loop(EARLY, CHUNKS, forward)
    full = gsum[7]
    b = 0
    for i in range(4):
        for j in range(i, 4):
            M[128 * i:128 * i + 128, 128 * j:128 * j + 128] = full[16 * b:16 * b + 16].reshape(128, 128) * (1.0 / ROWS)
            b += 1
    factor(M, R, W, wk, rk)
    out_r = pltpu.make_async_copy(R, r_out, osem.at[0])
    out_w = pltpu.make_async_copy(wp.at[0:2], w_out, osem.at[1])
    out_r.start()
    wp[0] = W[...].astype(BF16)
    wp[1] = (W[...] - wp[0].astype(F32)).astype(BF16)
    wp[2] = (W[...] - wp[0].astype(F32) - wp[1].astype(F32)).astype(BF16)
    out_w.start()

    last = (((1,), (1,)), ((), ()))

    def store_q(i):
        span = pl.ds(16 * i, 16)
        return pltpu.make_async_copy(qv.at[span], q_hbm.at[span], qsem.at[i])

    def form_basis():
        await_bytes(sr.at[:, 0:124], sp_r.at[0])

        def pick_block(i):
            at = at_s[0, i]
            for p in range(4):
                xs[i, :, 128 * p:128 * p + 128] = sr[p, at]

        loop(0, BLK_DEV, pick_block)
        def basis(i):
            span = pl.ds(16 * i, 16)
            rows = xs[span].reshape(512, 512)
            out = lax.dot_general(rows, wp[2], last, preferred_element_type=F32)
            out = out + lax.dot_general(rows, wp[1], last, preferred_element_type=F32)
            out = out + lax.dot_general(rows, wp[0], last, preferred_element_type=F32)
            qv[span] = out.reshape(16, 32, 512)
            store_q(i).start()

        loop(0, 4, basis)

    acc[...] = jnp.zeros((512, 512), F32)

    def cross_step(k):
        await_bytes(yr.at[0:3, pl.ds(16 * k, 16)], ys_r.at[k])
        acc[...] += lax.dot_general(panel_rows(xr, k), panel_rows(yr, k), contract, preferred_element_type=F32)

    loop(0, CHUNKS, cross_step)
    for j in range(4):
        csum[0][64 * j:64 * j + 64] = acc[:, 128 * j:128 * j + 128].reshape(64, 8, 128)

    def copy_half(src, dst):
        pltpu.make_async_copy(src, dst, osem.at[2]).start()

    drain_c = all_sum(C_GROUPS, *csum[:7], c_out, *csum[7:], keep=copy_half, after_scatter=form_basis)
    drain_g()
    drain_c()
    await_bytes(ids.at[0:31], id_s.at[0])
    await_bytes(sr.at[:, 0:124], sp_s.at[0])
    await_bytes(xo.at[0:3], xs_s.at[0])
    await_bytes(yo.at[0:3], ys_s.at[0])
    loop(0, 4, lambda i: store_q(i).wait())
    out_r.wait()
    out_w.wait()
    await_bytes(csum[2], osem.at[2])


def finish(q_in, r_in, w_in, c_in, q_out, r_out, p_out, qv, R, W, C, cp, p, qi, qo, ii, oo):
    get_c = pltpu.make_async_copy(c_in, C, ii.at[0])
    get_w = pltpu.make_async_copy(w_in, W, ii.at[1])
    get_r = pltpu.make_async_copy(r_in, R, ii.at[2])
    parts = [pl.ds(16 * i, 16) for i in range(4)]
    gets = [pltpu.make_async_copy(q_in.at[t], qv.at[t], qi.at[i]) for i, t in enumerate(parts)]
    puts = [pltpu.make_async_copy(qv.at[t], q_out.at[t], qo.at[i]) for i, t in enumerate(parts)]
    put_r = pltpu.make_async_copy(R, r_out, oo.at[0])
    put_p = pltpu.make_async_copy(p, p_out, oo.at[1])
    get_c.start()
    get_w.start()
    for copy in gets:
        copy.start()
    get_r.start()
    get_c.wait()
    for j in range(4):
        rows = C[64 * j:64 * j + 64].reshape(512, 128)
        span = slice(128 * j, 128 * j + 128)
        c1 = rows.astype(BF16)
        cp[0, :, span] = c1
        cp[1, :, span] = (rows - c1.astype(F32)).astype(BF16)
    get_w.wait()

    def term(i, j):
        return jnp.dot(W[i], cp[j], preferred_element_type=F32)

    for i in range(2):
        gets[i].wait()
        puts[i].start()
    p[...] = (term(1, 1) + term(1, 0) + term(0, 1) + term(0, 0)) * (1.0 / 512.0)
    put_p.start()
    for i in range(2, 4):
        gets[i].wait()
        puts[i].start()
    get_r.wait()
    put_r.start()
    for copy in puts:
        copy.wait()
    put_r.wait()
    put_p.wait()


def body(owned_x, owned_y, patch_dest):
    V = pl.BlockSpec(memory_space=pltpu.VMEM)
    A = pl.BlockSpec(memory_space=pl.ANY)
    dma = pltpu.SemaphoreType.DMA
    square = jax.ShapeDtypeStruct((512, 512), F32)
    panels = pltpu.VMEM((4, 128, 32, 128), BF16)
    basis, upper, inverse, cross = pl.pallas_call(
        whole,
        out_shape=(jax.ShapeDtypeStruct((BLK_DEV, 32, 512), F32), square, jax.ShapeDtypeStruct((2, 512, 512), BF16), jax.ShapeDtypeStruct((CT, 8, 128), F32)),
        in_specs=[V, A, A],
        out_specs=(A, A, A, A),
        scratch_shapes=[
            pltpu.VMEM((129, 128, 128), BF16),
            pltpu.VMEM((129, 128, 128), BF16),
            panels, panels, panels, panels, panels,
            pltpu.VMEM((BLK_DEV, 32, 512), BF16),
            pltpu.VMEM((BLK_DEV, 32, 512), F32),
            pltpu.VMEM((512, 512), F32),
            pltpu.VMEM((512, 512), F32),
            pltpu.VMEM((512, 512), F32),
            pltpu.VMEM((512, 512), F32),
            pltpu.VMEM((3, 512, 512), BF16),
            pltpu.VMEM((128, 128), F32),
            pltpu.VMEM((128, 128), F32),
            pltpu.VMEM((32, 8, 128), jnp.int32),
            pltpu.VMEM((8, 128), jnp.int32),
            pltpu.SMEM((8, 128), jnp.int32),
            pltpu.VMEM((8, 128), jnp.int32),
            pltpu.SMEM((8, 128), jnp.int32),
            dma((2,)), dma((2,)), dma((4,)), dma((3,)),
            dma((1,)), dma((CHUNKS,)), dma((1,)), dma((CHUNKS,)),
            dma((1,)), dma((1,)), dma((1,)), dma((1,)),
        ] + sum_scratch(G_GROUPS, True) + sum_scratch(C_GROUPS, False),
        compiler_params=pltpu.CompilerParams(
            collective_id=0, has_side_effects=True, vmem_limit_bytes=63 << 20
        ),
        name="window",
    )(patch_dest.reshape(1, 128), owned_x, owned_y)
    return pl.pallas_call(
        finish,
        out_shape=(jax.ShapeDtypeStruct((BLK_DEV, 32, 512), F32), square, square),
        in_specs=[A, A, A, A],
        out_specs=(A, A, A),
        scratch_shapes=[
            pltpu.VMEM((BLK_DEV, 32, 512), F32),
            pltpu.VMEM((512, 512), F32),
            pltpu.VMEM((2, 512, 512), BF16),
            pltpu.VMEM((CT, 8, 128), F32),
            pltpu.VMEM((2, 512, 512), BF16),
            pltpu.VMEM((512, 512), F32),
            dma((4,)), dma((4,)), dma((3,)), dma((2,)),
        ],
        compiler_params=pltpu.CompilerParams(vmem_limit_bytes=63 << 20),
        name="finish",
    )(basis, upper, inverse, cross)


def solution(mesh):
    in_specs = (P("space", None, "snap"), P("space", None, "snap"), P("space"))
    out_specs = (P("space", "snap", None), P(), P())
    return jax.shard_map(body, mesh=mesh, in_specs=in_specs, out_specs=out_specs, check_vma=False)
```

```python
import jax
import jax.numpy as jnp
from jax import lax
from jax.experimental import pallas as pl
from jax.experimental.pallas import tpu as pltpu
from jax.sharding import PartitionSpec as P

BLK_DEV = 64
HI = lax.Precision.HIGHEST

def small_inv(P, b):
    if b == 1:
        return [[1.0 / P[0][0]]]
    if b == 2:
        a, h, d = P[0][0], P[0][1], P[1][1]
        r = 1.0 / (a * d - h * h)
        return [[d * r, -h * r], [-h * r, a * r]]
    h = b // 2
    A = [[P[i][j] for j in range(h)] for i in range(h)]
    B = [[P[i][h + j] for j in range(h)] for i in range(h)]
    D = [[P[h + i][h + j] for j in range(h)] for i in range(h)]
    Ai = small_inv(A, h)
    AiB = [[sum(Ai[i][k] * B[k][j] for k in range(h)) for j in range(h)] for i in range(h)]
    S = [[None] * h for _ in range(h)]
    for i in range(h):
        for j in range(i, h):
            S[i][j] = D[i][j] - sum(B[k][i] * AiB[k][j] for k in range(h))
            S[j][i] = S[i][j]
    Si = small_inv(S, h)
    out = [[None] * b for _ in range(b)]
    BS = [[sum(AiB[i][k] * Si[k][j] for k in range(h)) for j in range(h)] for i in range(h)]
    for i in range(h):
        for j in range(h):
            out[h + i][h + j] = Si[i][j]
            out[i][h + j] = -BS[i][j]
            out[h + j][i] = -BS[i][j]
    for i in range(h):
        for j in range(i, h):
            v = Ai[i][j] + sum(BS[i][k] * AiB[j][k] for k in range(h))
            out[i][j] = v
            out[j][i] = v
    return out

def diag_block(D, b, r_out, w_out):
    lane = lax.broadcasted_iota(jnp.int32, (1, 128), 1)
    sub = lax.broadcasted_iota(jnp.int32, (8, 1), 0)
    M = list(D)
    for g in range(0, 128, b):
        v0, s0 = g // 8, g % 8
        r = [M[v0][s0 + s:s0 + s + 1, :] for s in range(b)]
        C0 = [jnp.broadcast_to(M[v0][:, g + t:g + t + 1], (8, 128)) for t in range(b)]
        P = [[C0[t][s0 + s:s0 + s + 1, :] for t in range(b)] for s in range(b)]
        ingroup = (lane >= g) & (lane < g + b)
        rp = [jnp.where(ingroup, jnp.where(lane == g + s, 1.0, 0.0), r[s]) for s in range(b)]
        if g + b < 128:
            Pi = small_inv(P, b)
            rt = [sum(Pi[s][t] * rp[t] for t in range(b)) for s in range(b)]
            for v in range(v0, 16):
                if v == v0 and s0 + b >= 8:
                    continue
                new = jnp.where(ingroup, 0.0, M[v])
                for s in range(b):
                    cs = C0[s] if v == v0 else M[v][:, g + s:g + s + 1]
                    new = new - cs * rt[s]
                if v == v0:
                    new = jnp.where(sub >= s0 + b, new, M[v])
                M[v] = new
        er, eb = list(r), list(rp)
        p = [list(row) for row in P]
        for s in range(b):
            sc = lax.rsqrt(p[s][s])
            for t in range(s + 1, b):
                m = p[s][t] / p[s][s]
                er[t] = er[t] - m * er[s]
                eb[t] = eb[t] - m * eb[s]
                for q in range(t, b):
                    p[t][q] = p[t][q] - m * p[s][q]
            r_out[g + s:g + s + 1, :] = jnp.where(lane >= g + s, er[s] * sc, 0.0)
            w_out[g + s:g + s + 1, :] = jnp.where(lane <= g + s, eb[s] * sc, 0.0)

def factor(M, R, W, wk, rk, nblk=4, b=4):
    n = nblk * 128
    colb = lax.broadcasted_iota(jnp.int32, (1, n), 1) // 128
    def outer(k, _):
        o = pl.multiple_of(k * 128, 128)
        kb = pl.ds(o, 128)
        D = [M[pl.ds(pl.multiple_of(o + 8 * v, 8), 8), kb] for v in range(16)]
        diag_block(D, b, rk, wk)
        M[kb, kb] = (lax.broadcasted_iota(jnp.int32, (128, 128), 0) == lax.broadcasted_iota(jnp.int32, (128, 128), 1)).astype(jnp.float32)
        row = jnp.dot(wk[...], M[kb, :], precision=HI, preferred_element_type=jnp.float32)
        M[kb, :] = row
        W[kb, :] = jnp.where(colb <= k, row, 0.0)
        R[kb, :] = jnp.where(colb > k, row, 0.0)
        R[kb, kb] = rk[...]
        def trail(i, _):
            ib = pl.ds(pl.multiple_of(i * 128, 128), 128)
            lik = M[kb, ib]
            upd = lax.dot_general(lik, M[kb, :], (((0,), (0,)), ((), ())), precision=HI, preferred_element_type=jnp.float32)
            M[ib, :] = jnp.where(colb == k, 0.0, M[ib, :]) - upd
            return 0
        lax.fori_loop(k + 1, nblk, trail, 0)
        return 0
    lax.fori_loop(0, nblk, outer, 0)


ROWS = 262144
MESH = pl.DeviceIdType.MESH
F32 = jnp.float32
BF16 = jnp.bfloat16
ORDER = (0, 2, 1, 3)
CHUNKS = 8
EARLY = 5
FIRST_Y = 2
CT = 256
G_GROUPS = ((0, 64), (64, 96))
C_GROUPS = ((0, 64), (64, 64), (128, 64), (192, 64))


def where_am_i():
    s = lax.axis_index("space")
    return s // 8, (s // 2) % 4, s % 2, lax.axis_index("snap"), s


def space_of(y, x, c):
    return (lax.rem(y, 4) * 4 + lax.rem(x, 4)) * 2 + lax.rem(c, 2)


def remote(src, dst, ss, rs, space=None, snap=None):
    dev = {}
    if space is not None:
        dev["space"] = space
    if snap is not None:
        dev["snap"] = snap
    return pltpu.make_async_remote_copy(
        src_ref=src, dst_ref=dst, send_sem=ss, recv_sem=rs, device_id=dev, device_id_type=MESH
    )


def loop(lo, hi, body):
    def step(i, carry):
        body(i)
        return carry

    lax.fori_loop(lo, hi, step, 0)


def await_bytes(ref, sem):
    pltpu.make_async_copy(ref, ref, sem).wait()


def column(row):
    eye = lax.broadcasted_iota(jnp.int32, (128, 128), 0) == lax.broadcasted_iota(jnp.int32, (128, 128), 1)
    return jnp.sum(jnp.where(eye, jnp.broadcast_to(row, (128, 128)), 0), axis=1, keepdims=True)


def slot_tables(dest, y, x, c):
    slab = jnp.where(dest >= 0, dest // BLK_DEV, -1)
    lane = lax.broadcasted_iota(jnp.int32, (128, 128), 1)
    sub = lax.broadcasted_iota(jnp.int32, (128, 128), 0)
    same = (column(slab) == slab) & (sub < lane)
    rank = jnp.sum(same.astype(jnp.int32), axis=0, keepdims=True)
    dy = (slab // 8 - y + 4) % 4
    dx = ((slab // 2) % 4 - x + 4) % 4
    dc = (slab % 2 - c + 2) % 2
    place = jnp.where(dy == 1, 2, jnp.where(dy == 2, 1, dy))
    pos = ((dc * 4 + (dx - dy + 4) % 4) * 4 + place) * 4 + rank
    pos = column(jnp.where(dest >= 0, pos, -1))
    hit = pos == lane
    slot = jnp.sum(jnp.where(hit, sub - 128, 0), axis=0, keepdims=True) + 128
    block = jnp.sum(jnp.where(hit, column(dest) + 1, 0), axis=0, keepdims=True) - 1
    return slot, block


def all_sum(groups, tiles, b1, half, b2, piece, zb, half2, full, ss, r1, r2, r3, r4, r5, keep, after_scatter=None, after_z=None):
    y, x, c, z, s = where_am_i()
    chip = s // 2
    mate = chip * 2 + (1 - c)

    def chip_at(d):
        return lax.rem(y + d // 4, 4) * 4 + lax.rem(x + lax.rem(d, 4), 4)

    spans = [(g, at, n // 2, n // 32) for g, (at, n) in enumerate(groups)]

    def swap(g, at, h, m):
        return remote(tiles.at[pl.ds(at + (1 - c) * h, h)], b1.at[at // 2:at // 2 + h], ss.at[0], r1.at[g], space=mate)

    def scatter(g, at, h, m, d):
        q = chip_at(d)
        return remote(half.at[pl.ds(at // 2 + q * m, m)], b2.at[chip, at // 32:at // 32 + m], ss.at[1], r2.at[g], space=q * 2 + c)

    def across(g, at, h, m, d):
        mine = pl.ds(at // 32, m)
        return remote(piece.at[mine], zb.at[z, mine], ss.at[2], r3.at[g], snap=lax.rem(z + d, 4))

    def gather(g, at, h, m, d):
        mine = pl.ds(at // 2 + chip * m, m)
        return remote(half2.at[mine], half2.at[mine], ss.at[3], r4.at[g], space=chip_at(d) * 2 + c)

    def swap_back(g, at, h, m):
        return remote(half2.at[at // 2:at // 2 + h], full.at[pl.ds(at + c * h, h)], ss.at[4], r5.at[g], space=mate)

    for sp in spans:
        swap(*sp).start()
    for sp in spans:
        g, at, h, m = sp
        swap(*sp).wait_recv()
        half[at // 2:at // 2 + h] = tiles[pl.ds(at + c * h, h)] + b1[at // 2:at // 2 + h]
        loop(1, 16, lambda d: scatter(*sp, d).start())
        b2[chip, at // 32:at // 32 + m] = half[pl.ds(at // 2 + chip * m, m)]
    if after_scatter is not None:
        after_scatter()
    for sp in spans:
        g, at, h, m = sp
        mine = slice(at // 32, at // 32 + m)
        await_bytes(b2.at[0:15, mine], r2.at[g])
        total = b2[0, mine]
        for q in range(1, 16):
            total = total + b2[q, mine]
        piece[mine] = total
        for d in (1, 2, 3):
            across(*sp, d).start()
        zb[z, mine] = piece[mine]
    if after_z is not None:
        after_z()
    for sp in spans:
        g, at, h, m = sp
        mine = slice(at // 32, at // 32 + m)
        await_bytes(zb.at[0:3, mine], r3.at[g])
        half2[pl.ds(at // 2 + chip * m, m)] = zb[0, mine] + zb[1, mine] + zb[2, mine] + zb[3, mine]
        loop(1, 16, lambda d: gather(*sp, d).start())
    for sp in spans:
        g, at, h, m = sp
        await_bytes(b2.at[0:15, at // 32:at // 32 + m], r4.at[g])
        swap_back(*sp).start()
        keep(half2.at[at // 2:at // 2 + h], full.at[pl.ds(at + c * h, h)])
    for sp in spans:
        swap_back(*sp).wait_recv()

    def drain():
        for stage, sent in enumerate((b1, b2.at[0:15], zb.at[0:3], b2.at[0:15], b1)):
            await_bytes(sent, ss.at[stage])

    return drain


def sum_scratch(groups, with_full):
    n = sum(size for _, size in groups)
    k = len(groups)
    h, m = n // 2, n // 32
    dma = pltpu.SemaphoreType.DMA
    return [
        pltpu.VMEM((n, 8, 128), F32),
        pltpu.VMEM((h, 8, 128), F32),
        pltpu.VMEM((h, 8, 128), F32),
        pltpu.VMEM((16, m, 8, 128), F32),
        pltpu.VMEM((m, 8, 128), F32),
        pltpu.VMEM((4, m, 8, 128), F32),
        pltpu.VMEM((h, 8, 128), F32),
    ] + [pltpu.VMEM((n, 8, 128), F32)] * with_full + [dma((5,))] + [dma((k,))] * 5


def whole(dest, x_hbm, y_hbm, q_hbm, r_out, w_out, c_out, xin, yin, xo, yo, xr, yr, sr, xs, qv, acc, M, W, R, wp, wk, rk,
          ids, tab_v, tab_s, at_v, at_s, lsem, tsem, qsem, osem, xs_s, xs_r, ys_s, ys_r, sp_s, sp_r, id_s, id_r, *sums):
    y, x, c, z, s = where_am_i()
    gsum, csum = sums[:14], sums[14:]
    load_x = pltpu.make_async_copy(x_hbm, xin.at[pl.ds(0, 128)], lsem.at[0])
    load_y = pltpu.make_async_copy(y_hbm, yin.at[pl.ds(0, 128)], lsem.at[1])
    load_x.start()
    load_y.start()

    def space_at(k, j):
        a = ORDER[j]
        return space_of(y + a, x + a + lax.rem(k, 4), c + k // 4)

    barrier = pltpu.get_barrier_semaphore()
    for o in range(1, 32):
        pl.semaphore_signal(barrier, inc=1, device_id={"space": space_at(o // 4, o % 4)}, device_id_type=MESH)
    for d in (1, 2, 3):
        pl.semaphore_signal(barrier, inc=1, device_id={"snap": lax.rem(z + d, 4)}, device_id_type=MESH)

    xin[128] = jnp.zeros((128, 128), BF16)
    yin[128] = jnp.zeros((128, 128), BF16)
    slot, block = slot_tables(dest[...], y, x, c)
    tab_v[...] = jnp.broadcast_to(jnp.clip(slot, 0, 128), (8, 128))
    ids[s] = jnp.broadcast_to(block, (8, 128))
    tab_copy = pltpu.make_async_copy(tab_v, tab_s, tsem.at[0])
    tab_copy.start()
    tab_copy.wait()
    load_x.wait()

    def order_slots(src, dst, recv, k):
        def one(i):
            got = src[tab_s[0, i]]
            for q in range(4):
                dst[q, i] = got[32 * q:32 * q + 32]
            recv[z, i] = dst[z, i]

        loop(16 * k, 16 * k + 16, one)

    def over_z(src, recv, ss, rs, k):
        span = pl.ds(16 * k, 16)
        out = []
        for d in (1, 2, 3):
            to = lax.rem(z + d, 4)
            out.append(remote(src.at[to, span], recv.at[z, span], ss.at[0], rs.at[k], snap=to))
        return out

    def send_z(src, recv, ss, rs, k):
        for cp in over_z(src, recv, ss, rs, k):
            cp.start()

    order_slots(xin, xo, xr, 0)
    pl.semaphore_wait(barrier, 34)
    for k in range(1, CHUNKS):
        order_slots(xin, xo, xr, k)
        send_z(xo, xr, xs_s, xs_r, k - 1)
    load_y.wait()
    order_slots(yin, yo, yr, 0)
    send_z(xo, xr, xs_s, xs_r, CHUNKS - 1)

    def send_ids(k, j):
        return remote(ids.at[s], ids.at[s], id_s.at[0], id_r.at[0], space=space_at(k, j))

    for o in range(1, 32):
        send_ids(o // 4, o % 4).start()
    loop(1, CHUNKS, lambda k: order_slots(yin, yo, yr, k))
    for k in range(FIRST_Y):
        send_z(yo, yr, ys_s, ys_r, k)

    await_bytes(ids.at[0:31], id_r.at[0])
    wanted = s * BLK_DEV + lax.broadcasted_iota(jnp.int32, (BLK_DEV, 1), 0)
    place = lax.rem(lax.broadcasted_iota(jnp.int32, (1, 128), 1), 4)
    found = jnp.zeros((BLK_DEV, 128), jnp.int32)
    for src in range(32):
        found = found + jnp.where(ids[src][0:1, :] == wanted, place + 4 * src, 0)
    found = jnp.sum(found, axis=1, keepdims=True)
    pick = lax.broadcasted_iota(jnp.int32, (BLK_DEV, 128), 0) == lax.broadcasted_iota(jnp.int32, (BLK_DEV, 128), 1)
    found = jnp.sum(jnp.where(pick, found, 0), axis=0, keepdims=True)
    at_v[...] = jnp.broadcast_to(jnp.clip(found, 0, 127), (8, 128))
    at_copy = pltpu.make_async_copy(at_v, at_s, tsem.at[1])
    at_copy.start()
    at_copy.wait()

    def to_slab(k, j):
        o = 4 * k + j
        return remote(xr.at[:, pl.ds(4 * o, 4)], sr.at[:, pl.ds(4 * s, 4)], sp_s.at[0], sp_r.at[0], space=space_at(k, j))

    def panel_rows(buf, k):
        return jnp.concatenate([buf[p, pl.ds(16 * k, 16)].reshape(512, 128) for p in range(4)], axis=1)

    acc[...] = jnp.zeros((512, 512), F32)
    contract = (((0,), (0,)), ((), ()))

    def forward(k):
        for j in range(4):
            to_slab(k, j).start()

    def gram_step(k):
        await_bytes(xr.at[0:3, pl.ds(16 * k, 16)], xs_r.at[k])

        @pl.when(k == 0)
        def _():
            sr[:, pl.ds(4 * s, 4)] = xr[:, 0:4]
            for j in range(1, 4):
                to_slab(0, j).start()

        @pl.when((k > 0) & (k < EARLY))
        def _():
            forward(k)

        rows = panel_rows(xr, k)
        acc[...] += lax.dot_general(rows, rows, contract, preferred_element_type=F32)

    loop(0, CHUNKS, gram_step)

    def later_y():
        for k in range(FIRST_Y, CHUNKS):
            send_z(yo, yr, ys_s, ys_r, k)

    b = 0
    for i in range(4):
        for j in range(i, 4):
            gsum[0][16 * b:16 * b + 16] = acc[128 * i:128 * i + 128, 128 * j:128 * j + 128].reshape(16, 8, 128)
            b += 1
    def store_half(src, dst):
        dst[...] = src[...]

    drain_g = all_sum(G_GROUPS, *gsum, keep=store_half, after_z=later_y)
    loop(EARLY, CHUNKS, forward)
    full = gsum[7]
    b = 0
    for i in range(4):
        for j in range(i, 4):
            M[128 * i:128 * i + 128, 128 * j:128 * j + 128] = full[16 * b:16 * b + 16].reshape(128, 128) * (1.0 / ROWS)
            b += 1
    factor(M, R, W, wk, rk)
    out_r = pltpu.make_async_copy(R, r_out, osem.at[0])
    out_w = pltpu.make_async_copy(wp.at[0:2], w_out, osem.at[1])
    out_r.start()
    wp[0] = W[...].astype(BF16)
    wp[1] = (W[...] - wp[0].astype(F32)).astype(BF16)
    wp[2] = (W[...] - wp[0].astype(F32) - wp[1].astype(F32)).astype(BF16)
    out_w.start()

    last = (((1,), (1,)), ((), ()))

    def store_q(i):
        span = pl.ds(16 * i, 16)
        return pltpu.make_async_copy(qv.at[span], q_hbm.at[span], qsem.at[i])

    def form_basis():
        await_bytes(sr.at[:, 0:124], sp_r.at[0])

        def pick_block(i):
            at = at_s[0, i]
            for p in range(4):
                xs[i, :, 128 * p:128 * p + 128] = sr[p, at]

        loop(0, BLK_DEV, pick_block)
        def basis(i):
            span = pl.ds(16 * i, 16)
            rows = xs[span].reshape(512, 512)
            out = lax.dot_general(rows, wp[2], last, preferred_element_type=F32)
            out = out + lax.dot_general(rows, wp[1], last, preferred_element_type=F32)
            out = out + lax.dot_general(rows, wp[0], last, preferred_element_type=F32)
            qv[span] = out.reshape(16, 32, 512)
            store_q(i).start()

        loop(0, 4, basis)

    acc[...] = jnp.zeros((512, 512), F32)

    def cross_step(k):
        await_bytes(yr.at[0:3, pl.ds(16 * k, 16)], ys_r.at[k])
        acc[...] += lax.dot_general(panel_rows(xr, k), panel_rows(yr, k), contract, preferred_element_type=F32)

    loop(0, CHUNKS, cross_step)
    for j in range(4):
        csum[0][64 * j:64 * j + 64] = acc[:, 128 * j:128 * j + 128].reshape(64, 8, 128)

    def copy_half(src, dst):
        pltpu.make_async_copy(src, dst, osem.at[2]).start()

    drain_c = all_sum(C_GROUPS, *csum[:7], c_out, *csum[7:], keep=copy_half, after_scatter=form_basis)
    drain_g()
    drain_c()
    await_bytes(ids.at[0:31], id_s.at[0])
    await_bytes(sr.at[:, 0:124], sp_s.at[0])
    await_bytes(xo.at[0:3], xs_s.at[0])
    await_bytes(yo.at[0:3], ys_s.at[0])
    loop(0, 4, lambda i: store_q(i).wait())
    out_r.wait()
    out_w.wait()
    await_bytes(csum[2], osem.at[2])


def finish(q_in, r_in, w_in, c_in, q_out, r_out, p_out, qv, R, W, C, cp, p, qi, qo, ii, oo):
    halves = [pl.ds(128 * i, 128) for i in range(2)]
    get_c = [pltpu.make_async_copy(c_in.at[t], C.at[t], ii.at[3 * i]) for i, t in enumerate(halves)]
    get_w = pltpu.make_async_copy(w_in, W, ii.at[1])
    get_r = pltpu.make_async_copy(r_in, R, ii.at[2])
    parts = [pl.ds(16 * i, 16) for i in range(4)]
    gets = [pltpu.make_async_copy(q_in.at[t], qv.at[t], qi.at[i]) for i, t in enumerate(parts)]
    puts = [pltpu.make_async_copy(qv.at[t], q_out.at[t], qo.at[i]) for i, t in enumerate(parts)]
    put_r = pltpu.make_async_copy(R, r_out, oo.at[0])
    sides = [slice(0, 256), slice(256, 512)]
    put_p = [pltpu.make_async_copy(p.at[:, t], p_out.at[:, t], oo.at[1 + i]) for i, t in enumerate(sides)]
    get_c[0].start()
    get_w.start()
    get_c[1].start()
    for copy in gets:
        copy.start()
    get_r.start()
    for i in range(2):
        get_c[i].wait()
        for j in (2 * i, 2 * i + 1):
            rows = C[64 * j:64 * j + 64].reshape(512, 128)
            span = slice(128 * j, 128 * j + 128)
            c1 = rows.astype(BF16)
            cp[0, :, span] = c1
            cp[1, :, span] = (rows - c1.astype(F32)).astype(BF16)
        if i == 0:
            get_w.wait()

        def term(a, b):
            return jnp.dot(W[a], cp[b, :, sides[i]], preferred_element_type=F32)

        p[:, sides[i]] = (term(1, 1) + term(1, 0) + term(0, 1) + term(0, 0)) * (1.0 / 512.0)
        put_p[i].start()
        for t in (2 * i, 2 * i + 1):
            gets[t].wait()
            puts[t].start()
    get_r.wait()
    put_r.start()
    for copy in puts:
        copy.wait()
    put_r.wait()
    for copy in put_p:
        copy.wait()


def body(owned_x, owned_y, patch_dest):
    V = pl.BlockSpec(memory_space=pltpu.VMEM)
    A = pl.BlockSpec(memory_space=pl.ANY)
    dma = pltpu.SemaphoreType.DMA
    square = jax.ShapeDtypeStruct((512, 512), F32)
    panels = pltpu.VMEM((4, 128, 32, 128), BF16)
    basis, upper, inverse, cross = pl.pallas_call(
        whole,
        out_shape=(jax.ShapeDtypeStruct((BLK_DEV, 32, 512), F32), square, jax.ShapeDtypeStruct((2, 512, 512), BF16), jax.ShapeDtypeStruct((CT, 8, 128), F32)),
        in_specs=[V, A, A],
        out_specs=(A, A, A, A),
        scratch_shapes=[
            pltpu.VMEM((129, 128, 128), BF16),
            pltpu.VMEM((129, 128, 128), BF16),
            panels, panels, panels, panels, panels,
            pltpu.VMEM((BLK_DEV, 32, 512), BF16),
            pltpu.VMEM((BLK_DEV, 32, 512), F32),
            pltpu.VMEM((512, 512), F32),
            pltpu.VMEM((512, 512), F32),
            pltpu.VMEM((512, 512), F32),
            pltpu.VMEM((512, 512), F32),
            pltpu.VMEM((3, 512, 512), BF16),
            pltpu.VMEM((128, 128), F32),
            pltpu.VMEM((128, 128), F32),
            pltpu.VMEM((32, 8, 128), jnp.int32),
            pltpu.VMEM((8, 128), jnp.int32),
            pltpu.SMEM((8, 128), jnp.int32),
            pltpu.VMEM((8, 128), jnp.int32),
            pltpu.SMEM((8, 128), jnp.int32),
            dma((2,)), dma((2,)), dma((4,)), dma((3,)),
            dma((1,)), dma((CHUNKS,)), dma((1,)), dma((CHUNKS,)),
            dma((1,)), dma((1,)), dma((1,)), dma((1,)),
        ] + sum_scratch(G_GROUPS, True) + sum_scratch(C_GROUPS, False),
        compiler_params=pltpu.CompilerParams(
            collective_id=0, has_side_effects=True, vmem_limit_bytes=63 << 20
        ),
        name="window",
    )(patch_dest.reshape(1, 128), owned_x, owned_y)
    return pl.pallas_call(
        finish,
        out_shape=(jax.ShapeDtypeStruct((BLK_DEV, 32, 512), F32), square, square),
        in_specs=[A, A, A, A],
        out_specs=(A, A, A),
        scratch_shapes=[
            pltpu.VMEM((BLK_DEV, 32, 512), F32),
            pltpu.VMEM((512, 512), F32),
            pltpu.VMEM((2, 512, 512), BF16),
            pltpu.VMEM((CT, 8, 128), F32),
            pltpu.VMEM((2, 512, 512), BF16),
            pltpu.VMEM((512, 512), F32),
            dma((4,)), dma((4,)), dma((4,)), dma((3,)),
        ],
        compiler_params=pltpu.CompilerParams(vmem_limit_bytes=63 << 20),
        name="finish",
    )(basis, upper, inverse, cross)


def solution(mesh):
    in_specs = (P("space", None, "snap"), P("space", None, "snap"), P("space"))
    out_specs = (P("space", "snap", None), P(), P())
    return jax.shard_map(body, mesh=mesh, in_specs=in_specs, out_specs=out_specs, check_vma=False)
```
